32 devices in a mesh: grp: 2 (over x), date: 8 (over z, y), pix: 2 (over core).
Axes of the slice: x: 2, y: 2, z: 4, core: 2. Of those that a mesh axis runs over, the one named last changes fastest.
Arguments:
- slc: bfloat16 [2, 160, 16, 256], P(None, ('grp', 'date'), None, 'pix'), parts along dimension 1, may hold values from -3 to 3
- pairs: int32 [224, 2], P('grp'), parts along dimension 0, may hold values from 0 to 79, as said below
Outputs:
- phases: float32 [2, 160, 16, 256], P(None, ('grp', 'date'), None, 'pix'), parts along dimension 1
The draws below stay inside these ranges and needn't reach their ends.
There are 2 independent parts, one for each index of `grp`. The reference program is written for one: setup_inputs(seed, part) draws one part's arguments, and reference() takes and returns one part's arrays. A program takes and returns all parts, laid end to end along the dimension named above; each array names one. Nothing has to cross between parts.
Inputs may be any that keep to these rules, and one draw needn't show every extreme that they name: `pairs`: each row is (i, j) with i < j <= i + 10; rows are distinct; at most 28 rows have i in one aligned block of 10 dates, and some block has exactly 28; some row has j = i + 10.
All inputs are finite; a program needn't handle non-finite values.
Results may differ from the reference program's by a relative error of at most 0.0003.
Values may be sent and summed in bfloat16 or wider, within the bound.
No kernel may reach another device: no remote copies, remote signals or barrier semaphores. Data moves between devices by JAX's collectives and lax.ppermute only.
A program may use at most 64 MiB of HBM per device.

```python
import math
import jax
import jax.numpy as jnp
from jax import lax

DATE_DEV = 10
GAP = 10
PAIR_DEV = 14
WIN = 2
COLS = 256
ITERS = 3
DATES = 80
PAIRS = 112
ROWS = 16


def draw_slc(key, part):
    subkeys = jax.random.split(jax.random.fold_in(key, 3), 7)
    grid_shape = (DATES, ROWS, COLS)
    common_amp = jnp.exp(jax.random.uniform(subkeys[0], (1, ROWS, COLS), jnp.float32, math.log(0.5), math.log(2.0)))
    date_amp = jnp.exp(jax.random.uniform(subkeys[1], grid_shape, jnp.float32, math.log(0.6), math.log(1.5)))
    rough_scale = jnp.exp(jax.random.uniform(subkeys[2], (1, ROWS, COLS), jnp.float32, math.log(0.1), math.log(2.0)))
    jitter = jax.random.normal(subkeys[3], grid_shape, jnp.float32)
    offset = jax.random.uniform(subkeys[4], (DATES, 1, 1), jnp.float32, -math.pi, math.pi)
    ramp_rate = 2.0 * jax.random.normal(subkeys[5], (DATES, 1, 1), jnp.float32)
    base_phase = jax.random.uniform(subkeys[6], (1, ROWS, COLS), jnp.float32, -math.pi, math.pi)
    columns = jnp.arange(COLS, dtype=jnp.float32) / COLS - 0.5
    angle_field = base_phase + offset + ramp_rate * columns[None, None, :] + rough_scale * jitter
    amplitude = common_amp * date_amp
    return jnp.stack([amplitude * jnp.cos(angle_field), amplitude * jnp.sin(angle_field)]).astype(jnp.bfloat16)


def draw_pairs(key, part):
    shards = DATES // DATE_DEV
    block_size = DATE_DEV * GAP
    cand_count = DATES * GAP
    candidate = jnp.arange(cand_count, dtype=jnp.int32)
    start_date = candidate // GAP
    step_gap = candidate % GAP + 1
    valid = start_date + step_gap < DATES
    subkeys = jax.random.split(jax.random.fold_in(key, 11), 3)
    ranks = jnp.concatenate([jax.random.permutation(subkeys[0], shards - 1).astype(jnp.int32) + 1, jnp.zeros((1,), jnp.int32)])
    spread = jnp.abs(2 * ranks - (shards - 1))
    counts = PAIR_DEV + jnp.where(2 * ranks > shards - 1, 1, -1) * (spread * PAIR_DEV // (shards - 1))
    scores = jax.random.randint(subkeys[1], (cand_count,), 0, 65536, jnp.int32) * cand_count + candidate
    scores = jnp.where(candidate % block_size == GAP - 1, 2 ** 30, scores)
    scores = jnp.where(valid, scores, -1)
    score_grid = scores.reshape(shards, block_size)
    ranking = jnp.argsort(-score_grid, axis=1)
    places = jnp.argsort(ranking, axis=1)
    chosen = (places < counts[:, None]) & valid.reshape(shards, block_size)
    picked = jnp.where(chosen.reshape(-1), jax.random.randint(subkeys[2], (cand_count,), 0, 65536, jnp.int32) * cand_count + candidate + 1, 0)
    chosen_rows = lax.top_k(picked, PAIRS)[1]
    return jnp.stack([start_date[chosen_rows], start_date[chosen_rows] + step_gap[chosen_rows]], axis=1).astype(jnp.int32)


def setup_inputs(seed: int = 0, part: int = 0) -> dict:
    key_list = jax.random.split(jax.random.key(seed), 3)
    part_keys = jax.random.split(jax.random.fold_in(key_list[2], part), 3)
    slc = draw_slc(jax.random.fold_in(jax.random.fold_in(key_list[2], part), 71), part)
    pairs = draw_pairs(jax.random.fold_in(jax.random.fold_in(key_list[2], part), 71), part)
    return {"slc": slc, "pairs": pairs}


def box_sum(values, margin):
    height = values.shape[-2] - 2 * margin
    breadth = values.shape[-1] - 2 * margin
    row_sums = values[..., 0:height, :]
    for offset in range(1, 2 * margin + 1):
        row_sums = row_sums + values[..., offset:offset + height, :]
    result = row_sums[..., 0:breadth]
    for offset in range(1, 2 * margin + 1):
        result = result + row_sums[..., offset:offset + breadth]
    return result

def coherence(first_tiles, second_tiles):
    first_re = first_tiles[0].astype(jnp.float32)
    first_im = first_tiles[1].astype(jnp.float32)
    second_re = second_tiles[0].astype(jnp.float32)
    second_im = second_tiles[1].astype(jnp.float32)
    cross_re = first_re * second_re + first_im * second_im
    cross_im = first_im * second_re - first_re * second_im
    power = first_re * first_re + first_im * first_im + second_re * second_re + second_im * second_im
    denom = box_sum(power, WIN)
    return (2.0 * box_sum(cross_re, WIN) / denom, 2.0 * box_sum(cross_im, WIN) / denom)

def normalize(summed):
    modulus = jnp.sqrt(summed[0] * summed[0] + summed[1] * summed[1])
    return summed / jnp.maximum(modulus, 1.0)[None]

def reference(slc, pairs):
    padded = jnp.pad(slc, ((0, 0), (0, 0), (WIN, WIN), (WIN, WIN)))

    def one_pair(pair_row):
        first_tiles = lax.dynamic_index_in_dim(padded, pair_row[0], axis=1, keepdims=True)
        second_tiles = lax.dynamic_index_in_dim(padded, pair_row[1], axis=1, keepdims=True)
        return coherence(first_tiles, second_tiles)
    coh_re, coh_im = lax.map(one_pair, pairs)
    coh_re = coh_re.reshape(PAIRS, ROWS * COLS)
    coh_im = coh_im.reshape(PAIRS, ROWS * COLS)
    first_dates = pairs[:, 0]
    second_dates = pairs[:, 1]
    phases = jnp.stack([jnp.ones((DATES, ROWS * COLS), jnp.float32), jnp.zeros((DATES, ROWS * COLS), jnp.float32)])
    for iteration in range(ITERS):
        at_far = jnp.take(phases, second_dates, axis=1)
        at_near = jnp.take(phases, first_dates, axis=1)
        fwd_re = coh_re * at_far[0] - coh_im * at_far[1]
        fwd_im = coh_re * at_far[1] + coh_im * at_far[0]
        bwd_re = coh_re * at_near[0] + coh_im * at_near[1]
        bwd_im = coh_re * at_near[1] - coh_im * at_near[0]
        summed_re = phases[0] + jax.ops.segment_sum(fwd_re, first_dates, num_segments=DATES) + jax.ops.segment_sum(bwd_re, second_dates, num_segments=DATES)
        summed_im = phases[1] + jax.ops.segment_sum(fwd_im, first_dates, num_segments=DATES) + jax.ops.segment_sum(bwd_im, second_dates, num_segments=DATES)
        phases = normalize(jnp.stack([summed_re, summed_im]))
    return phases.reshape(2, DATES, ROWS, COLS)
```

```python
import functools

import jax
import jax.numpy as jnp
from jax import lax
from jax.experimental import pallas as pl
from jax.experimental.pallas import tpu as pltpu
from jax.sharding import PartitionSpec as P

WIN = 2
ITERS = 3
GAP = 10
LANES = 128


def pack_edges(slc_ref, edge_ref):
    comps, dates, rows, cols = slc_ref.shape
    lead = (1 - lax.axis_index("pix")) * WIN
    lane = lax.broadcasted_iota(jnp.int32, (rows, cols), 1)
    acc = jnp.zeros((rows, cols), jnp.float32)
    for c in range(comps):
        for k in range(dates):
            place = WIN * (c * dates + k)
            tile = slc_ref[c, k].astype(jnp.float32)
            moved = pltpu.roll(tile, lead + place, 1)
            acc = jnp.where((lane >= place) & (lane < place + WIN), moved, acc)
    edge_ref[...] = acc.astype(edge_ref.dtype)


def link_kernel(
    pairs_ref, mine_ref, mate_ref, cross_ref, za_ref, zb_ref, out_ref,
    sre, sim, hre, him, power, are, aim, bre, bim, cre, cim, stage,
    list_i, list_j, second, third, *, unroll,
):
    _, dates, rows, cols = out_ref.shape
    tiles = 2 * dates + 1
    block = lax.axis_index("date")
    pix = lax.axis_index("pix")
    odd = block % 2
    far = (block // 2) % 2
    base = dates * (2 * (block // 2) - 3)
    own = (3 + odd) * dates
    lane = lax.broadcasted_iota(jnp.int32, (rows, cols), 1)
    outer = pix * (cols - WIN)
    facing = (lane >= outer) & (lane < outer + WIN)
    pitch = rows + 8
    stage[...] = jnp.zeros_like(stage)

    def box(center, halo, slot):
        total = center
        for shift in range(1, WIN + 1):
            left = jnp.where(lane < shift, halo, center)
            right = jnp.where(lane >= cols - shift, halo, center)
            total = total + pltpu.roll(left, cols - shift, 1)
            total = total + pltpu.roll(right, shift, 1)
        start = 8 + slot * pitch
        stage[pl.ds(start, rows), :] = total
        result = total
        for shift in range(1, WIN + 1):
            result = result + stage[pl.ds(start - shift, rows), :]
            result = result + stage[pl.ds(start + shift, rows), :]
        return result

    def load_block(ref, first, slot):
        edge = ref[first + tiles - 1].astype(jnp.float32)
        edge = pltpu.roll(edge, -WIN * pix & (cols - 1), 1)

        def one(step, carry):
            for u in range(2):
                k = step * 2 + u
                where = slot * dates + k
                re = ref[first + k].astype(jnp.float32)
                im = ref[first + dates + k].astype(jnp.float32)
                hr = jnp.where(facing, pltpu.roll(edge, -WIN * k & (cols - 1), 1), 0.0)
                hi = jnp.where(facing, pltpu.roll(edge, -WIN * (dates + k) & (cols - 1), 1), 0.0)
                sre[where] = re
                sim[where] = im
                hre[where] = hr
                him[where] = hi
                power[where] = box(re * re + im * im, hr * hr + hi * hi, u)
            return carry

        lax.fori_loop(0, dates // 2, one, 0)

    load_block(mine_ref, 0, 3 + odd)
    load_block(mate_ref, 0, 4 - odd)
    load_block(cross_ref, 0, 7 * odd)
    up, down = 5 - 4 * far, 1 + 4 * far
    load_block(za_ref, 0, up + odd)
    load_block(za_ref, tiles, up + 1 - odd)
    load_block(zb_ref, 0, down + odd)
    load_block(zb_ref, tiles, down + 1 - odd)

    def select(p, counts):
        n1, n2, n3 = counts
        i = pairs_ref[2 * p] - base
        j = pairs_ref[2 * p + 1] - base
        list_i[n1] = i
        list_j[n1] = j
        second[n2] = n1
        third[n3] = n1

        def within(reach):
            low, high = own - reach * dates, own + (reach + 1) * dates
            return ((j >= low) & (i < high)).astype(jnp.int32)

        return n1 + within(2), n2 + within(1), n3 + within(0)

    zero = jnp.int32(0)
    n1, n2, n3 = lax.fori_loop(0, pairs_ref.shape[0] // 2, select, (zero, zero, zero))

    def start(w, carry):
        are[w] = jnp.ones((rows, cols), jnp.float32)
        aim[w] = jnp.zeros((rows, cols), jnp.float32)
        return carry

    lax.fori_loop(0, are.shape[0], start, 0)

    def cohere(p, slot):
        i, j = list_i[p], list_j[p]

        def cross(fr, fi, sr, si):
            return fr * sr + fi * si, fi * sr - fr * si

        main = cross(sre[i], sim[i], sre[j], sim[j])
        rim = cross(hre[i], him[i], hre[j], him[j])
        scale = 2.0 / (power[i] + power[j])
        re = box(main[0], rim[0], 2 * slot) * scale
        im = box(main[1], rim[1], 2 * slot + 1) * scale
        cre[p] = re
        cim[p] = im
        are[i] = are[i] + re
        aim[i] = aim[i] + im
        are[j] = are[j] + re
        aim[j] = aim[j] - im

    def groups(count, width, body):
        def several(q, carry):
            for u in range(width):
                body(q * width + u, u)
            return carry

        whole = count // width
        lax.fori_loop(0, whole, several, 0)
        lax.fori_loop(whole * width, count, lambda p, carry: (body(p, 0), carry)[1], 0)

    groups(n1, unroll, cohere)

    def normal(w, xr, xi, yr, yi):
        re, im = xr[w], xi[w]
        scale = lax.rsqrt(jnp.maximum(re * re + im * im, 1.0))
        re, im = re * scale, im * scale
        xr[w] = re
        xi[w] = im
        yr[w] = re
        yi[w] = im

    def step(index, count, xr, xi, yr, yi):
        def one(q, u):
            p = index[q]
            i, j = list_i[p], list_j[p]
            re, im = cre[p], cim[p]
            nr, ni, fr, fi = xr[i], xi[i], xr[j], xi[j]
            yr[i] = yr[i] + (re * fr - im * fi)
            yi[i] = yi[i] + (re * fi + im * fr)
            yr[j] = yr[j] + (re * nr + im * ni)
            yi[j] = yi[j] + (re * ni - im * nr)

        groups(count, unroll, one)

    def settle(low, count, xr, xi, yr, yi):
        def two(q, carry):
            for u in range(2):
                normal(low + 2 * q + u, xr, xi, yr, yi)
            return carry

        lax.fori_loop(0, count // 2, two, 0)

    settle(own - 2 * dates, 5 * dates, are, aim, bre, bim)
    step(second, n2, are, aim, bre, bim)
    settle(own - dates, 3 * dates, bre, bim, are, aim)
    step(third, n3, bre, bim, are, aim)

    def finish(k, carry):
        re, im = are[own + k], aim[own + k]
        scale = lax.rsqrt(jnp.maximum(re * re + im * im, 1.0))
        out_ref[0, k] = re * scale
        out_ref[1, k] = im * scale
        return carry

    lax.fori_loop(0, dates, finish, 0)


def swap(array, axis, matching):
    return lax.ppermute(array, axis, [*matching, *((j, i) for i, j in matching)])


def on_device(slc, pairs):
    comps, dates, rows, cols = slc.shape
    size = lax.axis_size("date")
    pair_count = pairs.shape[0]
    assert lax.axis_size("pix") == 2 and size % 2 == 0 and cols == LANES
    assert GAP <= dates and dates % 2 == 0 and comps * dates * WIN <= cols and rows % 8 == 0

    vmem = pl.BlockSpec(memory_space=pltpu.VMEM)
    edge = pl.pallas_call(
        pack_edges,
        out_shape=jax.ShapeDtypeStruct((rows, cols), slc.dtype),
        in_specs=[vmem],
        out_specs=vmem,
    )(slc)
    edge = swap(edge, "pix", [(0, 1)])
    mine = jnp.concatenate([slc.reshape(comps * dates, rows, cols), edge[None]], axis=0)

    def matching(step, keep):
        return [(i, i + step) for i in range(size - step) if keep(i)]

    cross = swap(mine, "date", matching(3, lambda i: i % 2 == 1))
    mate = swap(mine, "date", matching(1, lambda i: i % 2 == 0))
    both = jnp.concatenate([mine, mate], axis=0)
    za = swap(both, "date", matching(2, lambda i: i // 2 % 2 == 0))
    zb = swap(both, "date", matching(2, lambda i: i // 2 % 2 == 1))

    window = 8 * dates
    unroll = max(1, 64 // rows)
    field = pltpu.VMEM((window, rows, cols), jnp.float32)
    pair_field = pltpu.VMEM((pair_count, rows, cols), jnp.float32)
    stage = pltpu.VMEM((8 + 2 * unroll * (rows + 8) + 8, cols), jnp.float32)
    index = pltpu.SMEM((pair_count,), jnp.int32)
    return pl.pallas_call(
        functools.partial(link_kernel, unroll=unroll),
        out_shape=jax.ShapeDtypeStruct((comps, dates, rows, cols), jnp.float32),
        in_specs=[pl.BlockSpec(memory_space=pltpu.SMEM)] + [vmem] * 5,
        out_specs=vmem,
        scratch_shapes=[field] * 9 + [pair_field] * 2 + [stage] + [index] * 4,
        compiler_params=pltpu.CompilerParams(vmem_limit_bytes=60 * 1024 * 1024),
    )(pairs.reshape(-1), mine, mate, cross, za, zb)


def solution(mesh):
    in_specs = (P(None, ("grp", "date"), None, "pix"), P("grp", None))
    out_specs = P(None, ("grp", "date"), None, "pix")
    return jax.shard_map(
        on_device, mesh=mesh, in_specs=in_specs, out_specs=out_specs, check_vma=False
    )
```

```python
import functools

import jax
import jax.numpy as jnp
from jax import lax
from jax.experimental import pallas as pl
from jax.experimental.pallas import tpu as pltpu
from jax.sharding import PartitionSpec as P

WIN = 2
ITERS = 3
GAP = 10
LANES = 128


def pack_edges(slc_ref, edge_ref):
    tiles, rows, cols = slc_ref.shape
    lead = (1 - lax.axis_index("pix")) * WIN
    lane = lax.broadcasted_iota(jnp.int32, (rows, cols), 1)
    acc = jnp.zeros((rows, cols), jnp.float32)
    for t in range(tiles):
        moved = pltpu.roll(slc_ref[t].astype(jnp.float32), lead + WIN * t, 1)
        acc = jnp.where((lane >= WIN * t) & (lane < WIN * (t + 1)), moved, acc)
    edge_ref[...] = acc.astype(edge_ref.dtype)


def place():
    block = lax.axis_index("date")
    return block % 2, (block // 2) % 2, block // 2


def make_box(rows, cols, stage):
    lane = lax.broadcasted_iota(jnp.int32, (rows, cols), 1)
    pitch = rows + 8

    def box(center, halo, slot):
        total = center
        for shift in range(1, WIN + 1):
            left = jnp.where(lane < shift, halo, center)
            right = jnp.where(lane >= cols - shift, halo, center)
            total = total + pltpu.roll(left, cols - shift, 1)
            total = total + pltpu.roll(right, shift, 1)
        start = 8 + slot * pitch
        stage[pl.ds(start, rows), :] = total
        result = total
        for shift in range(1, WIN + 1):
            result = result + stage[pl.ds(start - shift, rows), :]
            result = result + stage[pl.ds(start + shift, rows), :]
        return result

    return box


def loader(dates, rows, cols, width, box, fields):
    sre, sim, hre, him, power = fields
    pix = lax.axis_index("pix")
    outer = pix * (cols - WIN)
    lane = lax.broadcasted_iota(jnp.int32, (rows, cols), 1)
    facing = (lane >= outer) & (lane < outer + WIN)

    def load(ref, first, edge, target):
        edge = pltpu.roll(edge.astype(jnp.float32), -WIN * pix & (cols - 1), 1)

        def one(step, carry):
            for u in range(width):
                k = step * width + u
                where = target + k
                re = ref[first + k].astype(jnp.float32)
                im = ref[first + dates + k].astype(jnp.float32)
                hr = jnp.where(facing, pltpu.roll(edge, -WIN * k & (cols - 1), 1), 0.0)
                hi = jnp.where(facing, pltpu.roll(edge, -WIN * (dates + k) & (cols - 1), 1), 0.0)
                sre[where] = re
                sim[where] = im
                hre[where] = hr
                him[where] = hi
                power[where] = box(re * re + im * im, hr * hr + hi * hi, u)
            return carry

        lax.fori_loop(0, dates // width, one, 0)

    return load


def coherer(box, fields, sums, offset, list_i, list_j, cre, cim, width):
    sre, sim, hre, him, power = fields
    are, aim = sums

    def cross(fr, fi, sr, si):
        return fr * sr + fi * si, fi * sr - fr * si

    def several(first):
        results = []
        for u in range(width):
            i, j = list_i[first + u] - offset, list_j[first + u] - offset
            main = cross(sre[i], sim[i], sre[j], sim[j])
            rim = cross(hre[i], him[i], hre[j], him[j])
            scale = 2.0 / (power[i] + power[j])
            re = box(main[0], rim[0], 2 * u) * scale
            im = box(main[1], rim[1], 2 * u + 1) * scale
            results.append((i, j, re, im))
        for u, (i, j, re, im) in enumerate(results):
            cre[first + u] = re
            cim[first + u] = im
            ri, rj, ii, ij = are[i], are[j], aim[i], aim[j]
            are[i] = ri + re
            are[j] = rj + re
            aim[i] = ii + im
            aim[j] = ij - im

    return several


def groups(first, count, width, body):
    def one(q, carry):
        body(first + q * width)
        return carry

    lax.fori_loop(0, (count + width - 1) // width, one, 0)


def near_kernel(
    pairs_ref, mine_ref, mate_ref, edge_mine_ref, edge_mate_ref,
    list_i, list_j, second, third, counts, sre, sim, hre, him, power, are, aim, cre, cim,
    stage, *, dates, unroll, width,
):
    _, rows, cols = sre.shape
    odd, _, chip = place()
    base = dates * (2 * chip - 3)
    own = (3 + odd) * dates
    inner = 3 * dates
    stage[...] = jnp.zeros_like(stage)
    box = make_box(rows, cols, stage)
    fields = (sre, sim, hre, him, power)
    load = loader(dates, rows, cols, width, box, fields)
    load(mine_ref, 0, edge_mine_ref[...], odd * dates)
    load(mate_ref, 0, edge_mate_ref[...], (1 - odd) * dates)

    def init(w, carry):
        are[w] = jnp.ones((rows, cols), jnp.float32)
        aim[w] = jnp.zeros((rows, cols), jnp.float32)
        return carry

    lax.fori_loop(0, 2 * dates, init, 0)

    def selection(inside):
        def one(p, found):
            n1, n2, n3 = found
            i = pairs_ref[2 * p] - base
            j = pairs_ref[2 * p + 1] - base
            local = ((i >= inner) & (j < inner + 2 * dates)).astype(jnp.int32)
            wanted = local if inside else 1 - local

            def within(reach):
                low, high = own - reach * dates, own + (reach + 1) * dates
                return wanted * ((j >= low) & (i < high)).astype(jnp.int32)

            list_i[n1] = i
            list_j[n1] = j
            second[n2] = n1
            third[n3] = n1
            return n1 + within(2), n2 + within(1), n3 + within(0)

        def four(q, found):
            for u in range(4):
                found = one(4 * q + u, found)
            return found

        def run(found):
            total = pairs_ref.shape[0] // 2
            found = lax.fori_loop(0, total // 4, four, found)
            return lax.fori_loop(total // 4 * 4, total, one, found)

        return run

    def pad(first, slot):
        for u in range(unroll):
            list_i[first + u] = slot
            list_j[first + u] = slot

    zero = jnp.int32(0)
    found = selection(True)((zero, zero, zero))
    pad(found[0], inner + 2 * dates)
    counts[0] = found[0]
    groups(
        0, found[0], unroll,
        coherer(box, fields, (are, aim), inner, list_i, list_j, cre, cim, unroll),
    )
    n1, n2, n3 = selection(False)(found)
    pad(n1, 8 * dates)
    for u in range(unroll):
        second[n2 + u] = n1
        third[n3 + u] = n1
    counts[1] = n1
    counts[2] = n2
    counts[3] = n3


def link_kernel(
    list_i, list_j, second, third, counts, cross_ref, za_ref, zb_ref,
    nsre, nsim, nhre, nhim, npower, nare, naim, ncre, ncim, out_ref,
    sre, sim, hre, him, power, are, aim, bre, bim, cre, cim, stage, *, unroll, width,
):
    _, dates, rows, cols = out_ref.shape
    tiles = 2 * dates + 1
    odd, far, _ = place()
    own = (3 + odd) * dates
    inner = 3 * dates
    stage[...] = jnp.zeros_like(stage)
    box = make_box(rows, cols, stage)
    fields = (sre, sim, hre, him, power)
    load = loader(dates, rows, cols, width, box, fields)
    local, n1, n2, n3 = counts[0], counts[1], counts[2], counts[3]

    def carry_over(k, carry):
        sources = (nsre, nsim, nhre, nhim, npower, nare, naim)
        for source, target in zip(sources, (*fields, are, aim), strict=True):
            target[inner + k] = source[k]
        return carry

    lax.fori_loop(0, 2 * dates, carry_over, 0)

    def keep(p, carry):
        cre[p] = ncre[p]
        cim[p] = ncim[p]
        return carry

    lax.fori_loop(0, local, keep, 0)

    def init(w, carry):
        for slot in (w, w + 5 * dates):
            are[slot] = jnp.ones((rows, cols), jnp.float32)
            aim[slot] = jnp.zeros((rows, cols), jnp.float32)
        return carry

    lax.fori_loop(0, 3 * dates, init, 0)

    load(cross_ref, 0, cross_ref[tiles - 1], 7 * odd * dates)
    up, down = 5 - 4 * far, 1 + 4 * far
    load(za_ref, 0, za_ref[tiles - 1], (up + odd) * dates)
    load(za_ref, tiles, za_ref[2 * tiles - 1], (up + 1 - odd) * dates)
    load(zb_ref, 0, zb_ref[tiles - 1], (down + odd) * dates)
    load(zb_ref, tiles, zb_ref[2 * tiles - 1], (down + 1 - odd) * dates)

    groups(
        local, n1 - local, unroll,
        coherer(box, fields, (are, aim), 0, list_i, list_j, cre, cim, unroll),
    )

    def scaled(re, im):
        scale = lax.rsqrt(jnp.maximum(re * re + im * im, 1.0))
        return re * scale, im * scale

    def settle(low, count, xr, xi, yr, yi):
        def one(q, carry):
            for u in range(width):
                w = low + width * q + u
                re, im = scaled(xr[w], xi[w])
                xr[w] = re
                xi[w] = im
                yr[w] = re
                yi[w] = im
            return carry

        lax.fori_loop(0, count // width, one, 0)

    def step(index, count, xr, xi, yr, yi):
        def several(first):
            for u in range(unroll):
                p = index[first + u]
                i, j = list_i[p], list_j[p]
                re, im = cre[p], cim[p]
                nr, ni, fr, fi = xr[i], xi[i], xr[j], xi[j]
                ri, rj, ii, ij = yr[i], yr[j], yi[i], yi[j]
                yr[i] = ri + (re * fr - im * fi)
                yr[j] = rj + (re * nr + im * ni)
                yi[i] = ii + (re * fi + im * fr)
                yi[j] = ij + (re * ni - im * nr)

        groups(0, count, unroll, several)

    settle(own - 2 * dates, 5 * dates, are, aim, bre, bim)
    step(second, n2, are, aim, bre, bim)
    settle(own - dates, 3 * dates, bre, bim, are, aim)
    step(third, n3, bre, bim, are, aim)
    for k in range(dates):
        re, im = scaled(are[own + k], aim[own + k])
        out_ref[0, k] = re
        out_ref[1, k] = im


def swap(array, axis, matching):
    return lax.ppermute(array, axis, [*matching, *((j, i) for i, j in matching)])


def on_device(slc, pairs):
    comps, dates, rows, cols = slc.shape
    size = lax.axis_size("date")
    pair_count = pairs.shape[0]
    assert lax.axis_size("pix") == 2 and size % 2 == 0 and cols == LANES
    assert GAP <= dates and dates % 2 == 0 and comps * dates * WIN <= cols and rows % 8 == 0

    vmem = pl.BlockSpec(memory_space=pltpu.VMEM)
    smem = pl.BlockSpec(memory_space=pltpu.SMEM)

    def held(array):
        return pltpu.with_memory_space_constraint(array, pltpu.VMEM)

    def matching(step, keep):
        return [(i, i + step) for i in range(size - step) if keep(i)]

    main = slc.reshape(comps * dates, rows, cols)
    mates = matching(1, lambda i: i % 2 == 0)
    mate = swap(main, "date", mates)
    edge = pl.pallas_call(
        pack_edges,
        out_shape=pltpu.VMEM((rows, cols), slc.dtype),
        in_specs=[vmem],
        out_specs=vmem,
    )(held(main))
    edge_mine = swap(edge, "pix", [(0, 1)])
    edge_mate = swap(edge, ("date", "pix"), [(2 * i + p, 2 * j + 1 - p) for i, j in mates for p in (0, 1)])
    cross = jnp.concatenate([main, edge_mine[None]], axis=0)
    both = jnp.concatenate([cross, mate, edge_mate[None]], axis=0)
    cross = swap(cross, "date", matching(3, lambda i: i % 2 == 1))
    za = swap(both, "date", matching(2, lambda i: i // 2 % 2 == 0))
    zb = swap(both, "date", matching(2, lambda i: i // 2 % 2 == 1))

    unroll = max(1, 128 // rows)
    width = max(w for w in range(1, unroll + 1) if dates % w == 0)
    per_block = min(pair_count, 2 * pair_count // size)
    local_cap = min(pair_count, 2 * per_block) + unroll
    cap = min(pair_count, 6 * per_block) + unroll
    window = 8 * dates + 1
    stage = pltpu.VMEM((16 + max(width, 2 * unroll) * (rows + 8), cols), jnp.float32)
    index = jax.ShapeDtypeStruct((pair_count + unroll,), jnp.int32)
    plane = 4 * rows * cols
    spare = 4 * 1024 * 1024 + 64 * plane
    local = pl.pallas_call(
        functools.partial(near_kernel, dates=dates, unroll=unroll, width=width),
        out_shape=[index] * 4
        + [jax.ShapeDtypeStruct((4,), jnp.int32)]
        + [pltpu.VMEM((2 * dates + 1, rows, cols), jnp.float32)] * 7
        + [pltpu.VMEM((local_cap, rows, cols), jnp.float32)] * 2,
        in_specs=[smem] + [vmem] * 4,
        out_specs=[smem] * 5 + [vmem] * 9,
        scratch_shapes=[stage],
        compiler_params=pltpu.CompilerParams(vmem_limit_bytes=spare),
    )(pairs.reshape(-1), held(main), held(mate), held(edge_mine), held(edge_mate))
    field = pltpu.VMEM((window, rows, cols), jnp.float32)
    pair_field = pltpu.VMEM((cap, rows, cols), jnp.float32)
    return pl.pallas_call(
        functools.partial(link_kernel, unroll=unroll, width=width),
        out_shape=jax.ShapeDtypeStruct((comps, dates, rows, cols), jnp.float32),
        in_specs=[smem] * 5 + [vmem] * 12,
        out_specs=vmem,
        scratch_shapes=[field] * 9 + [pair_field] * 2 + [stage],
        compiler_params=pltpu.CompilerParams(vmem_limit_bytes=spare + (9 * window + 2 * cap) * plane),
    )(*local[:5], held(cross), held(za), held(zb), *(held(v) for v in local[5:]))


def solution(mesh):
    in_specs = (P(None, ("grp", "date"), None, "pix"), P("grp", None))
    out_specs = P(None, ("grp", "date"), None, "pix")
    return jax.shard_map(
        on_device, mesh=mesh, in_specs=in_specs, out_specs=out_specs, check_vma=False
    )
```

```python
import functools

import jax
import jax.numpy as jnp
from jax import lax
from jax.experimental import pallas as pl
from jax.experimental.pallas import tpu as pltpu
from jax.sharding import PartitionSpec as P

WIN = 2
ITERS = 3
GAP = 10
LANES = 128


def pack_edges(slc_ref, edge_ref):
    tiles, rows, cols = slc_ref.shape
    lead = (1 - lax.axis_index("pix")) * WIN
    lane = lax.broadcasted_iota(jnp.int32, (rows, cols), 1)
    acc = jnp.zeros((rows, cols), jnp.float32)
    for t in range(tiles):
        moved = pltpu.roll(slc_ref[t].astype(jnp.float32), lead + WIN * t, 1)
        acc = jnp.where((lane >= WIN * t) & (lane < WIN * (t + 1)), moved, acc)
    edge_ref[...] = acc.astype(edge_ref.dtype)


def place():
    block = lax.axis_index("date")
    return block % 2, (block // 2) % 2, block // 2


def select_kernel(pairs_ref, list_i, list_j, second, third, counts, band_ref, *, dates, unroll, local_cap):
    cols = band_ref.shape[1]
    odd, _, chip = place()
    base = dates * (2 * chip - 3)
    own = base + (3 + odd) * dates
    inner = base + 3 * dates
    row = lax.broadcasted_iota(jnp.int32, band_ref.shape, 0)
    column = lax.broadcasted_iota(jnp.int32, band_ref.shape, 1)
    apart = jnp.where(row < cols, row, row - 2 * cols * lax.axis_index("pix")) - column
    band_ref[...] = jnp.where((apart <= WIN) & (apart >= -WIN), 1.0, 0.0).astype(band_ref.dtype)

    def one(p, found):
        near, other, n2, n3 = found
        i, j = pairs_ref[2 * p], pairs_ref[2 * p + 1]

        def within(low, high):
            return ((j >= low) & (i < high)).astype(jnp.int32)

        local = ((i >= inner) & (j < inner + 2 * dates)).astype(jnp.int32)
        where = jnp.where(local == 1, near, other)
        list_i[where] = i - base
        list_j[where] = j - base
        second[n2] = where
        third[n3] = where
        return (
            near + local,
            other + (1 - local) * within(own - 2 * dates, own + 3 * dates),
            n2 + within(own - dates, own + 2 * dates),
            n3 + within(own, own + dates),
        )

    def four(q, found):
        for u in range(4):
            found = one(4 * q + u, found)
        return found

    zero = jnp.int32(0)
    total = pairs_ref.shape[0] // 2
    found = (zero, jnp.int32(local_cap), zero, zero)
    found = lax.fori_loop(0, total // 4, four, found)
    near, other, n2, n3 = lax.fori_loop(total // 4 * 4, total, one, found)
    for u in range(unroll):
        list_i[near + u] = 5 * dates
        list_j[near + u] = 5 * dates
        list_i[other + u] = 8 * dates
        list_j[other + u] = 8 * dates
        second[n2 + u] = other
        third[n3 + u] = other
    counts[0] = near
    counts[1] = other - local_cap
    counts[2] = n2
    counts[3] = n3


def make_boxes(rows, stage, band_ref):
    pitch = rows + 8

    def boxes(centers, halos):
        values = jnp.concatenate([jnp.concatenate(centers, axis=0), jnp.concatenate(halos, axis=0)], axis=1)
        high = values.astype(jnp.bfloat16)
        low = (values - high.astype(jnp.float32)).astype(jnp.bfloat16)
        band = band_ref[...]
        wide = jnp.dot(high, band, preferred_element_type=jnp.float32)
        wide = wide + jnp.dot(low, band, preferred_element_type=jnp.float32)
        results = []
        for slot in range(len(centers)):
            start = 8 + slot * pitch
            result = wide[slot * rows : (slot + 1) * rows]
            stage[pl.ds(start, rows), :] = result
            for shift in range(1, WIN + 1):
                result = result + stage[pl.ds(start - shift, rows), :]
                result = result + stage[pl.ds(start + shift, rows), :]
            results.append(result)
        return results

    return boxes


def loader(dates, cols, width, boxes, fields):
    sre, sim, hre, him, power = fields
    pix = lax.axis_index("pix")

    def load(ref, first, edge, target):
        edge = pltpu.roll(edge.astype(jnp.float32), -WIN * pix & (cols - 1), 1)
        for start in range(0, dates, width):
            squares, rims = [], []
            for k in range(start, start + width):
                re = ref[first + k].astype(jnp.float32)
                im = ref[first + dates + k].astype(jnp.float32)
                hr = pltpu.roll(edge, -WIN * k & (cols - 1), 1)
                hi = pltpu.roll(edge, -WIN * (dates + k) & (cols - 1), 1)
                sre[target + k] = re
                sim[target + k] = im
                hre[target + k] = hr
                him[target + k] = hi
                squares.append(re * re + im * im)
                rims.append(hr * hr + hi * hi)
            for u, value in enumerate(boxes(squares, rims)):
                power[target + start + u] = value

    return load


def coherer(boxes, fields, sums, offset, list_i, list_j, cre, cim, width):
    sre, sim, hre, him, power = fields
    are, aim = sums

    def cross(fr, fi, sr, si):
        return [fr * sr + fi * si, fi * sr - fr * si]

    def several(first):
        ends, centers, halos, scales = [], [], [], []
        for u in range(width):
            i, j = list_i[first + u] - offset, list_j[first + u] - offset
            ends.append((i, j))
            centers += cross(sre[i], sim[i], sre[j], sim[j])
            halos += cross(hre[i], him[i], hre[j], him[j])
            scales.append(2.0 / (power[i] + power[j]))
        sums_of = boxes(centers, halos)
        for u, (i, j) in enumerate(ends):
            re, im = sums_of[2 * u] * scales[u], sums_of[2 * u + 1] * scales[u]
            cre[first + u] = re
            cim[first + u] = im
            ri, rj, ii, ij = are[i], are[j], aim[i], aim[j]
            are[i] = ri + re
            are[j] = rj + re
            aim[i] = ii + im
            aim[j] = ij - im

    return several


def groups(first, count, width, body):
    def one(q, carry):
        body(first + q * width)
        return carry

    lax.fori_loop(0, (count + width - 1) // width, one, 0)


def near_kernel(
    list_i, list_j, counts, band_ref, mine_ref, mate_ref, edge_mine_ref, edge_mate_ref,
    sre, sim, hre, him, power, are, aim, cre, cim, stage, *, dates, unroll, width,
):
    _, rows, cols = sre.shape
    odd, _, _ = place()
    stage[...] = jnp.zeros_like(stage)
    boxes = make_boxes(rows, stage, band_ref)
    fields = (sre, sim, hre, him, power)
    load = loader(dates, cols, width, boxes, fields)
    load(mine_ref, 0, edge_mine_ref[...], odd * dates)
    load(mate_ref, 0, edge_mate_ref[...], (1 - odd) * dates)
    are[...] = jnp.ones_like(are)
    aim[...] = jnp.zeros_like(aim)
    groups(
        0, counts[0], unroll,
        coherer(boxes, fields, (are, aim), 3 * dates, list_i, list_j, cre, cim, unroll),
    )


def link_kernel(
    list_i, list_j, second, third, counts, band_ref, cross_ref, za_ref, zb_ref,
    nsre, nsim, nhre, nhim, npower, nare, naim, ncre, ncim, out_ref,
    sre, sim, hre, him, power, are, aim, bre, bim, cre, cim, stage, *, unroll, width, local_cap,
):
    _, dates, rows, cols = out_ref.shape
    tiles = 2 * dates + 1
    odd, far, _ = place()
    own = (3 + odd) * dates
    inner = 3 * dates
    stage[...] = jnp.zeros_like(stage)
    boxes = make_boxes(rows, stage, band_ref)
    fields = (sre, sim, hre, him, power)
    load = loader(dates, cols, width, boxes, fields)
    local, others, n2, n3 = counts[0], counts[1], counts[2], counts[3]

    sources = (nsre, nsim, nhre, nhim, npower, nare, naim)
    for source, target in zip(sources, (*fields, are, aim), strict=True):
        target[pl.ds(inner, 2 * dates)] = source[pl.ds(0, 2 * dates)]
    for low in (0, inner + 2 * dates):
        are[pl.ds(low, inner)] = jnp.ones((inner, rows, cols), jnp.float32)
        aim[pl.ds(low, inner)] = jnp.zeros((inner, rows, cols), jnp.float32)

    def keep(first):
        for u in range(unroll):
            cre[first + u] = ncre[first + u]
            cim[first + u] = ncim[first + u]

    groups(0, local, unroll, keep)

    load(cross_ref, 0, cross_ref[tiles - 1], 7 * odd * dates)
    up, down = 5 - 4 * far, 1 + 4 * far
    load(za_ref, 0, za_ref[tiles - 1], (up + odd) * dates)
    load(za_ref, tiles, za_ref[2 * tiles - 1], (up + 1 - odd) * dates)
    load(zb_ref, 0, zb_ref[tiles - 1], (down + odd) * dates)
    load(zb_ref, tiles, zb_ref[2 * tiles - 1], (down + 1 - odd) * dates)

    groups(
        local_cap, others, unroll,
        coherer(boxes, fields, (are, aim), 0, list_i, list_j, cre, cim, unroll),
    )

    def scaled(re, im):
        scale = lax.rsqrt(jnp.maximum(re * re + im * im, 1.0))
        return re * scale, im * scale

    def settle(low, count, xr, xi, yr, yi):
        def one(q, carry):
            for u in range(width):
                w = low + width * q + u
                re, im = scaled(xr[w], xi[w])
                xr[w] = re
                xi[w] = im
                yr[w] = re
                yi[w] = im
            return carry

        lax.fori_loop(0, count // width, one, 0)

    def step(index, count, xr, xi, yr, yi):
        def several(first):
            for u in range(unroll):
                p = index[first + u]
                i, j = list_i[p], list_j[p]
                re, im = cre[p], cim[p]
                nr, ni, fr, fi = xr[i], xi[i], xr[j], xi[j]
                ri, rj, ii, ij = yr[i], yr[j], yi[i], yi[j]
                yr[i] = ri + (re * fr - im * fi)
                yr[j] = rj + (re * nr + im * ni)
                yi[i] = ii + (re * fi + im * fr)
                yi[j] = ij + (re * ni - im * nr)

        groups(0, count, unroll, several)

    settle(own - 2 * dates, 5 * dates, are, aim, bre, bim)
    step(second, n2, are, aim, bre, bim)
    settle(own - dates, 3 * dates, bre, bim, are, aim)
    step(third, n3, bre, bim, are, aim)
    for k in range(dates):
        re, im = scaled(are[own + k], aim[own + k])
        out_ref[0, k] = re
        out_ref[1, k] = im


def swap(array, axis, matching):
    return lax.ppermute(array, axis, [*matching, *((j, i) for i, j in matching)])


def on_device(slc, pairs):
    comps, dates, rows, cols = slc.shape
    size = lax.axis_size("date")
    pair_count = pairs.shape[0]
    assert lax.axis_size("pix") == 2 and size % 2 == 0 and cols == LANES
    assert GAP <= dates and dates % 2 == 0 and comps * dates * WIN <= cols and rows % 8 == 0

    vmem = pl.BlockSpec(memory_space=pltpu.VMEM)
    smem = pl.BlockSpec(memory_space=pltpu.SMEM)

    def held(array):
        return pltpu.with_memory_space_constraint(array, pltpu.VMEM)

    def matching(step, keep):
        return [(i, i + step) for i in range(size - step) if keep(i)]

    main = slc.reshape(comps * dates, rows, cols)
    mates = matching(1, lambda i: i % 2 == 0)
    with jax.named_scope("mate"):
        mate = swap(main, "date", mates)
    edge = pl.pallas_call(
        pack_edges,
        out_shape=pltpu.VMEM((rows, cols), slc.dtype),
        in_specs=[vmem],
        out_specs=vmem,
    )(held(main))
    with jax.named_scope("edges"):
        edge_mine = swap(edge, "pix", [(0, 1)])
        edge_mate = swap(edge, ("date", "pix"), [(2 * i + p, 2 * j + 1 - p) for i, j in mates for p in (0, 1)])
    cross = jnp.concatenate([main, edge_mine[None]], axis=0)
    both = jnp.concatenate([cross, mate, edge_mate[None]], axis=0)
    with jax.named_scope("cross"):
        cross = swap(cross, "date", matching(3, lambda i: i % 2 == 1))
    with jax.named_scope("even"):
        za = swap(both, "date", matching(2, lambda i: i // 2 % 2 == 0))
    with jax.named_scope("odd"):
        zb = swap(both, "date", matching(2, lambda i: i // 2 % 2 == 1))

    unroll = max(1, 128 // rows)
    width = max(w for w in range(1, 2 * unroll + 1) if dates % w == 0)
    per_block = min(pair_count, 2 * pair_count // size)
    local_cap = min(pair_count, 2 * per_block) + unroll
    cap = local_cap + min(pair_count, 6 * per_block) + unroll
    window = 8 * dates + 1
    stage = pltpu.VMEM((16 + max(width, 2 * unroll) * (rows + 8), cols), jnp.float32)
    plane = 4 * rows * cols
    spare = 4 * 1024 * 1024 + 64 * plane
    lists = pl.pallas_call(
        functools.partial(select_kernel, dates=dates, unroll=unroll, local_cap=local_cap),
        out_shape=[pltpu.SMEM((n,), jnp.int32) for n in (cap, cap, pair_count + unroll, pair_count + unroll, 4)]
        + [pltpu.VMEM((2 * cols, cols), jnp.bfloat16)],
        in_specs=[smem],
        out_specs=[smem] * 5 + [vmem],
    )(pairs.reshape(-1))
    band = held(lists[5])
    lists = [pltpu.with_memory_space_constraint(v, pltpu.SMEM) for v in lists[:5]]
    local = pl.pallas_call(
        functools.partial(near_kernel, dates=dates, unroll=unroll, width=width),
        out_shape=[pltpu.VMEM((2 * dates + 1, rows, cols), jnp.float32)] * 7
        + [pltpu.VMEM((local_cap, rows, cols), jnp.float32)] * 2,
        in_specs=[smem] * 3 + [vmem] * 5,
        out_specs=[vmem] * 9,
        scratch_shapes=[stage],
        compiler_params=pltpu.CompilerParams(vmem_limit_bytes=spare),
    )(lists[0], lists[1], lists[4], band, held(main), held(mate), held(edge_mine), held(edge_mate))
    field = pltpu.VMEM((window, rows, cols), jnp.float32)
    pair_field = pltpu.VMEM((cap, rows, cols), jnp.float32)
    return pl.pallas_call(
        functools.partial(link_kernel, unroll=unroll, width=width, local_cap=local_cap),
        out_shape=jax.ShapeDtypeStruct((comps, dates, rows, cols), jnp.float32),
        in_specs=[smem] * 5 + [vmem] * 13,
        out_specs=vmem,
        scratch_shapes=[field] * 9 + [pair_field] * 2 + [stage],
        compiler_params=pltpu.CompilerParams(vmem_limit_bytes=spare + (9 * window + 2 * cap) * plane),
    )(*lists, band, held(cross), held(za), held(zb), *(held(v) for v in local))


def solution(mesh):
    in_specs = (P(None, ("grp", "date"), None, "pix"), P("grp", None))
    out_specs = P(None, ("grp", "date"), None, "pix")
    return jax.shard_map(
        on_device, mesh=mesh, in_specs=in_specs, out_specs=out_specs, check_vma=False
    )
```

```python
import functools

import jax
import jax.numpy as jnp
from jax import lax
from jax.experimental import pallas as pl
from jax.experimental.pallas import tpu as pltpu
from jax.sharding import PartitionSpec as P


WIN = 2
GAP = 10
LANES = 128


def pack_edges(slc_ref, near_ref, edge_ref):
    tiles, rows, cols = slc_ref.shape
    lead = (1 - lax.axis_index("pix")) * WIN
    lane = lax.broadcasted_iota(jnp.int32, (rows, cols), 1)
    acc = jnp.zeros((rows, cols), jnp.float32)
    for t in range(tiles):
        moved = pltpu.roll(slc_ref[t].astype(jnp.float32), lead + WIN * t, 1)
        acc = jnp.where((lane >= WIN * t) & (lane < WIN * (t + 1)), moved, acc)
    near_ref[...] = slc_ref[...]
    edge_ref[...] = acc.astype(edge_ref.dtype)


def place():
    block = lax.axis_index("date")
    return block % 2, (block // 2) % 2, block // 2


def select_kernel(pairs_ref, list_i, list_j, second, third, counts, band_ref, *, dates, unroll, local_cap):
    cols = band_ref.shape[1]
    odd, _, chip = place()
    base = dates * (2 * chip - 3)
    own = base + (3 + odd) * dates
    inner = base + 3 * dates
    row = lax.broadcasted_iota(jnp.int32, band_ref.shape, 0)
    column = lax.broadcasted_iota(jnp.int32, band_ref.shape, 1)
    apart = jnp.where(row < cols, row, row - 2 * cols * lax.axis_index("pix")) - column
    band_ref[...] = jnp.where((apart <= WIN) & (apart >= -WIN), 1.0, 0.0).astype(band_ref.dtype)

    def one(p, found):
        near, other, n2, n3 = found
        i, j = pairs_ref[2 * p], pairs_ref[2 * p + 1]

        def within(low, high):
            return ((j >= low) & (i < high)).astype(jnp.int32)

        local = ((i >= inner) & (j < inner + 2 * dates)).astype(jnp.int32)
        where = jnp.where(local == 1, near, other)
        list_i[where] = i - base
        list_j[where] = j - base
        second[n2] = where
        third[n3] = where
        return (
            near + local,
            other + (1 - local) * within(own - 2 * dates, own + 3 * dates),
            n2 + within(own - dates, own + 2 * dates),
            n3 + within(own, own + dates),
        )

    def four(q, found):
        for u in range(4):
            found = one(4 * q + u, found)
        return found

    zero = jnp.int32(0)
    total = pairs_ref.shape[0] // 2
    found = (zero, jnp.int32(local_cap), zero, zero)
    found = lax.fori_loop(0, total // 4, four, found)
    near, other, n2, n3 = lax.fori_loop(total // 4 * 4, total, one, found)
    for u in range(unroll):
        list_i[near + u] = 5 * dates
        list_j[near + u] = 5 * dates
        list_i[other + u] = 8 * dates
        list_j[other + u] = 8 * dates
        second[n2 + u] = other
        third[n3 + u] = other
    counts[0] = near
    counts[1] = other - local_cap
    counts[2] = n2
    counts[3] = n3


def make_boxes(rows, stage, band_ref):
    pitch = rows + 8

    def boxes(centers, halos):
        values = jnp.concatenate([jnp.concatenate(centers, axis=0), jnp.concatenate(halos, axis=0)], axis=1)
        high = values.astype(jnp.bfloat16)
        low = (values - high.astype(jnp.float32)).astype(jnp.bfloat16)
        band = band_ref[...]
        wide = jnp.dot(high, band, preferred_element_type=jnp.float32)
        wide = wide + jnp.dot(low, band, preferred_element_type=jnp.float32)
        results = []
        for slot in range(len(centers)):
            start = 8 + slot * pitch
            result = wide[slot * rows : (slot + 1) * rows]
            stage[pl.ds(start, rows), :] = result
            for shift in range(1, WIN + 1):
                result = result + stage[pl.ds(start - shift, rows), :]
                result = result + stage[pl.ds(start + shift, rows), :]
            results.append(result)
        return results

    return boxes


def loader(dates, cols, width, boxes, fields):
    sre, sim, hre, him, power = fields
    pix = lax.axis_index("pix")

    def load(ref, first, edge, target):
        edge = pltpu.roll(edge.astype(jnp.float32), -WIN * pix & (cols - 1), 1)
        for start in range(0, dates, width):
            squares, rims = [], []
            for k in range(start, start + width):
                re = ref[first + k].astype(jnp.float32)
                im = ref[first + dates + k].astype(jnp.float32)
                hr = pltpu.roll(edge, -WIN * k & (cols - 1), 1)
                hi = pltpu.roll(edge, -WIN * (dates + k) & (cols - 1), 1)
                sre[target + k] = re
                sim[target + k] = im
                hre[target + k] = hr
                him[target + k] = hi
                squares.append(re * re + im * im)
                rims.append(hr * hr + hi * hi)
            for u, value in enumerate(boxes(squares, rims)):
                power[target + start + u] = value

    return load


def coherer(boxes, fields, sums, offset, list_i, list_j, cre, cim, width):
    sre, sim, hre, him, power = fields
    are, aim = sums

    def cross(fr, fi, sr, si):
        return [fr * sr + fi * si, fi * sr - fr * si]

    def several(first):
        ends, centers, halos, scales = [], [], [], []
        for u in range(width):
            i, j = list_i[first + u] - offset, list_j[first + u] - offset
            ends.append((i, j))
            centers += cross(sre[i], sim[i], sre[j], sim[j])
            halos += cross(hre[i], him[i], hre[j], him[j])
            scales.append(2.0 / (power[i] + power[j]))
        sums_of = boxes(centers, halos)
        for u, (i, j) in enumerate(ends):
            re, im = sums_of[2 * u] * scales[u], sums_of[2 * u + 1] * scales[u]
            cre[first + u] = re
            cim[first + u] = im
            ri, rj, ii, ij = are[i], are[j], aim[i], aim[j]
            are[i] = ri + re
            are[j] = rj + re
            aim[i] = ii + im
            aim[j] = ij - im

    return several


def groups(first, count, width, body):
    def one(q, carry):
        body(first + q * width)
        return carry

    lax.fori_loop(0, (count + width - 1) // width, one, 0)


def near_kernel(
    list_i, list_j, counts, band_ref, mine_ref, mate_ref, edge_mine_ref, edge_mate_ref,
    sre, sim, hre, him, power, are, aim, cre, cim, stage, *, dates, unroll, width,
):
    _, rows, cols = sre.shape
    odd, _, _ = place()
    stage[...] = jnp.zeros_like(stage)
    boxes = make_boxes(rows, stage, band_ref)
    fields = (sre, sim, hre, him, power)
    load = loader(dates, cols, width, boxes, fields)
    load(mine_ref, 0, edge_mine_ref[...], odd * dates)
    load(mate_ref, 0, edge_mate_ref[...], (1 - odd) * dates)
    are[...] = jnp.ones_like(are)
    aim[...] = jnp.zeros_like(aim)
    groups(
        0, counts[0], unroll,
        coherer(boxes, fields, (are, aim), 3 * dates, list_i, list_j, cre, cim, unroll),
    )


def link_kernel(
    list_i, list_j, second, third, counts, band_ref, cross_ref, za_ref, zb_ref,
    nsre, nsim, nhre, nhim, npower, nare, naim, ncre, ncim, out_ref,
    sre, sim, hre, him, power, are, aim, bre, bim, cre, cim, stage, *, unroll, width, local_cap,
):
    _, dates, rows, cols = out_ref.shape
    tiles = 2 * dates + 1
    odd, far, _ = place()
    own = (3 + odd) * dates
    inner = 3 * dates
    stage[...] = jnp.zeros_like(stage)
    boxes = make_boxes(rows, stage, band_ref)
    fields = (sre, sim, hre, him, power)
    load = loader(dates, cols, width, boxes, fields)
    local, others, n2, n3 = counts[0], counts[1], counts[2], counts[3]

    sources = (nsre, nsim, nhre, nhim, npower, nare, naim)
    for source, target in zip(sources, (*fields, are, aim), strict=True):
        target[pl.ds(inner, 2 * dates)] = source[pl.ds(0, 2 * dates)]
    for low in (0, inner + 2 * dates):
        are[pl.ds(low, inner)] = jnp.ones((inner, rows, cols), jnp.float32)
        aim[pl.ds(low, inner)] = jnp.zeros((inner, rows, cols), jnp.float32)

    def keep(first):
        for u in range(unroll):
            cre[first + u] = ncre[first + u]
            cim[first + u] = ncim[first + u]

    groups(0, local, unroll, keep)

    load(cross_ref, 0, cross_ref[tiles - 1], 7 * odd * dates)
    up, down = 5 - 4 * far, 1 + 4 * far
    load(za_ref, 0, za_ref[tiles - 1], (up + odd) * dates)
    load(za_ref, tiles, za_ref[2 * tiles - 1], (up + 1 - odd) * dates)
    load(zb_ref, 0, zb_ref[tiles - 1], (down + odd) * dates)
    load(zb_ref, tiles, zb_ref[2 * tiles - 1], (down + 1 - odd) * dates)

    groups(
        local_cap, others, unroll,
        coherer(boxes, fields, (are, aim), 0, list_i, list_j, cre, cim, unroll),
    )

    def scaled(re, im):
        scale = lax.rsqrt(jnp.maximum(re * re + im * im, 1.0))
        return re * scale, im * scale

    def settle(low, count, xr, xi, yr, yi):
        def one(q, carry):
            for u in range(width):
                w = low + width * q + u
                re, im = scaled(xr[w], xi[w])
                xr[w] = re
                xi[w] = im
                yr[w] = re
                yi[w] = im
            return carry

        lax.fori_loop(0, count // width, one, 0)

    def step(index, count, xr, xi, yr, yi):
        def several(first):
            for u in range(unroll):
                p = index[first + u]
                i, j = list_i[p], list_j[p]
                re, im = cre[p], cim[p]
                nr, ni, fr, fi = xr[i], xi[i], xr[j], xi[j]
                ri, rj, ii, ij = yr[i], yr[j], yi[i], yi[j]
                yr[i] = ri + (re * fr - im * fi)
                yr[j] = rj + (re * nr + im * ni)
                yi[i] = ii + (re * fi + im * fr)
                yi[j] = ij + (re * ni - im * nr)

        groups(0, count, unroll, several)

    settle(own - 2 * dates, 5 * dates, are, aim, bre, bim)
    step(second, n2, are, aim, bre, bim)
    settle(own - dates, 3 * dates, bre, bim, are, aim)
    step(third, n3, bre, bim, are, aim)
    for k in range(dates):
        re, im = scaled(are[own + k], aim[own + k])
        out_ref[0, k] = re
        out_ref[1, k] = im


def swap(array, axis, matching):
    return lax.ppermute(array, axis, [*matching, *((j, i) for i, j in matching)])


def on_device(slc, pairs):
    comps, dates, rows, cols = slc.shape
    size = lax.axis_size("date")
    pair_count = pairs.shape[0]
    assert lax.axis_size("pix") == 2 and size % 2 == 0 and cols == LANES
    assert GAP <= dates and dates % 2 == 0 and comps * dates * WIN <= cols and rows % 8 == 0

    vmem = pl.BlockSpec(memory_space=pltpu.VMEM)
    smem = pl.BlockSpec(memory_space=pltpu.SMEM)

    def held(array):
        return pltpu.with_memory_space_constraint(array, pltpu.VMEM)

    def matching(step, keep):
        return [(i, i + step) for i in range(size - step) if keep(i)]

    main = slc.reshape(comps * dates, rows, cols)
    mates = matching(1, lambda i: i % 2 == 0)
    mate = swap(main, "date", mates)
    near, edge = pl.pallas_call(
        pack_edges,
        out_shape=[pltpu.VMEM(main.shape, slc.dtype), pltpu.VMEM((rows, cols), slc.dtype)],
        in_specs=[vmem],
        out_specs=[vmem] * 2,
    )(main)
    edge_mine = swap(edge, "pix", [(0, 1)])
    edge_mate = swap(edge, ("date", "pix"), [(2 * i + p, 2 * j + 1 - p) for i, j in mates for p in (0, 1)])
    cross = jnp.concatenate([near, edge_mine[None]], axis=0)
    both = jnp.concatenate([cross, mate, edge_mate[None]], axis=0)
    cross = swap(cross, "date", matching(3, lambda i: i % 2 == 1))
    za = swap(both, "date", matching(2, lambda i: i // 2 % 2 == 0))
    zb = swap(both, "date", matching(2, lambda i: i // 2 % 2 == 1))

    unroll = max(1, 128 // rows)
    width = max(w for w in range(1, 2 * unroll + 1) if dates % w == 0)
    per_block = min(pair_count, 2 * pair_count // size)
    local_cap = min(pair_count, 2 * per_block) + unroll
    cap = local_cap + min(pair_count, 6 * per_block) + unroll
    window = 8 * dates + 1
    stage = pltpu.VMEM((16 + max(width, 2 * unroll) * (rows + 8), cols), jnp.float32)
    plane = 4 * rows * cols
    spare = 4 * 1024 * 1024 + 64 * plane
    lists = pl.pallas_call(
        functools.partial(select_kernel, dates=dates, unroll=unroll, local_cap=local_cap),
        out_shape=[pltpu.SMEM((n,), jnp.int32) for n in (cap, cap, pair_count + unroll, pair_count + unroll, 4)]
        + [pltpu.VMEM((2 * cols, cols), jnp.bfloat16)],
        in_specs=[smem],
        out_specs=[smem] * 5 + [vmem],
    )(pairs.reshape(-1))
    band = held(lists[5])
    lists = [pltpu.with_memory_space_constraint(v, pltpu.SMEM) for v in lists[:5]]
    local = pl.pallas_call(
        functools.partial(near_kernel, dates=dates, unroll=unroll, width=width),
        out_shape=[pltpu.VMEM((2 * dates + 1, rows, cols), jnp.float32)] * 7
        + [pltpu.VMEM((local_cap, rows, cols), jnp.float32)] * 2,
        in_specs=[smem] * 3 + [vmem] * 5,
        out_specs=[vmem] * 9,
        scratch_shapes=[stage],
        compiler_params=pltpu.CompilerParams(vmem_limit_bytes=spare),
    )(lists[0], lists[1], lists[4], band, held(near), held(mate), held(edge_mine), held(edge_mate))
    field = pltpu.VMEM((window, rows, cols), jnp.float32)
    pair_field = pltpu.VMEM((cap, rows, cols), jnp.float32)
    return pl.pallas_call(
        functools.partial(link_kernel, unroll=unroll, width=width, local_cap=local_cap),
        out_shape=jax.ShapeDtypeStruct((comps, dates, rows, cols), jnp.float32),
        in_specs=[smem] * 5 + [vmem] * 13,
        out_specs=vmem,
        scratch_shapes=[field] * 9 + [pair_field] * 2 + [stage],
        compiler_params=pltpu.CompilerParams(vmem_limit_bytes=spare + (9 * window + 2 * cap) * plane),
    )(*lists, band, held(cross), held(za), held(zb), *(held(v) for v in local))


def solution(mesh):
    in_specs = (P(None, ("grp", "date"), None, "pix"), P("grp", None))
    out_specs = P(None, ("grp", "date"), None, "pix")

    return jax.shard_map(
        on_device, mesh=mesh, in_specs=in_specs, out_specs=out_specs, check_vma=False
    )
```

```python
import functools

import jax
import jax.numpy as jnp
from jax import lax
from jax.experimental import pallas as pl
from jax.experimental.pallas import tpu as pltpu
from jax.sharding import PartitionSpec as P


WIN = 2
GAP = 10
LANES = 128
SPARE = 3


def pack_edges(slc_ref, near_ref, edge_ref):
    tiles, rows, cols = slc_ref.shape
    lead = (1 - lax.axis_index("pix")) * WIN
    lane = lax.broadcasted_iota(jnp.int32, (rows, cols), 1)
    acc = jnp.zeros((rows, cols), jnp.float32)
    for t in range(tiles):
        moved = pltpu.roll(slc_ref[t].astype(jnp.float32), lead + WIN * t, 1)
        acc = jnp.where((lane >= WIN * t) & (lane < WIN * (t + 1)), moved, acc)
    near_ref[...] = slc_ref[...]
    edge_ref[...] = acc.astype(edge_ref.dtype)


def place():
    block = lax.axis_index("date")
    return block % 2, (block // 2) % 2, block // 2


def select_kernel(pairs_ref, list_i, list_j, second, third, counts, band_ref, *, dates, unroll, local_cap):
    cols = band_ref.shape[1]
    odd, _, chip = place()
    base = dates * (2 * chip - 3)
    own = base + (3 + odd) * dates
    inner = base + 3 * dates
    row = lax.broadcasted_iota(jnp.int32, band_ref.shape, 0)
    column = lax.broadcasted_iota(jnp.int32, band_ref.shape, 1)
    apart = jnp.where(row < cols, row, row - 2 * cols * lax.axis_index("pix")) - column
    band_ref[...] = jnp.where((apart <= WIN) & (apart >= -WIN), 1.0, 0.0).astype(band_ref.dtype)

    def one(p, found):
        near, other, n2, n3 = found
        i, j = pairs_ref[0, p], pairs_ref[1, p]

        def within(low, high):
            return ((j >= low) & (i < high)).astype(jnp.int32)

        local = ((i >= inner) & (j < inner + 2 * dates)).astype(jnp.int32)
        where = jnp.where(local == 1, near, other)
        list_i[where] = i - base
        list_j[where] = j - base
        second[n2] = where
        third[n3] = where
        return (
            near + local,
            other + (1 - local) * within(own - 2 * dates, own + 3 * dates),
            n2 + within(own - dates, own + 2 * dates),
            n3 + within(own, own + dates),
        )

    def four(q, found):
        for u in range(4):
            found = one(4 * q + u, found)
        return found

    zero = jnp.int32(0)
    total = pairs_ref.shape[1]
    found = (zero, jnp.int32(local_cap), zero, zero)
    found = lax.fori_loop(0, total // 4, four, found)
    near, other, n2, n3 = lax.fori_loop(total // 4 * 4, total, one, found)
    for u in range(SPARE * unroll):
        list_i[near + u] = 8 * dates
        list_j[near + u] = 8 * dates
        list_i[other + u] = 8 * dates
        list_j[other + u] = 8 * dates
    for u in range(unroll):
        second[n2 + u] = other
        third[n3 + u] = other
    counts[0] = near
    counts[1] = other - local_cap
    counts[2] = n2
    counts[3] = n3


def make_boxes(rows, stage, band_ref):
    pitch = rows + 8

    def spread(centers, halos, slot):
        values = jnp.concatenate([jnp.concatenate(centers, axis=0), jnp.concatenate(halos, axis=0)], axis=1)
        high = values.astype(jnp.bfloat16)
        low = (values - high.astype(jnp.float32)).astype(jnp.bfloat16)
        band = band_ref[...]
        wide = jnp.dot(high, band, preferred_element_type=jnp.float32)
        wide = wide + jnp.dot(low, band, preferred_element_type=jnp.float32)
        for k in range(len(centers)):
            stage[pl.ds(8 + (slot + k) * pitch, rows), :] = wide[k * rows : (k + 1) * rows]

    def gather(slot):
        start = 8 + slot * pitch
        result = stage[pl.ds(start, rows), :]
        for shift in range(1, WIN + 1):
            result = result + stage[pl.ds(start - shift, rows), :]
            result = result + stage[pl.ds(start + shift, rows), :]
        return result

    return spread, gather


def loader(dates, cols, width, boxes, fields):
    sre, sim, hre, him, power = fields
    spread, gather = boxes
    pix = lax.axis_index("pix")

    def load(ref, first, edge, target):
        edge = pltpu.roll(edge.astype(jnp.float32), -WIN * pix & (cols - 1), 1)
        for start in range(0, dates, width):
            squares, rims = [], []
            for k in range(start, start + width):
                re = ref[first + k].astype(jnp.float32)
                im = ref[first + dates + k].astype(jnp.float32)
                hr = pltpu.roll(edge, -WIN * k & (cols - 1), 1)
                hi = pltpu.roll(edge, -WIN * (dates + k) & (cols - 1), 1)
                sre[target + k] = re
                sim[target + k] = im
                hre[target + k] = hr
                him[target + k] = hi
                squares.append(re * re + im * im)
                rims.append(hr * hr + hi * hi)
            spread(squares, rims, 0)
            for u in range(width):
                power[target + start + u] = gather(u)

    return load


def cohere(boxes, fields, sums, list_i, list_j, cre, cim, first, count, width):
    sre, sim, hre, him, power = fields
    are, aim = sums
    spread, gather = boxes

    def cross(fr, fi, sr, si):
        return [fr * sr + fi * si, fi * sr - fr * si]

    def multiply(group, half):
        centers, halos = [], []
        for u in range(width):
            p = first + group * width + u
            i, j = list_i[p], list_j[p]
            centers += cross(sre[i], sim[i], sre[j], sim[j])
            halos += cross(hre[i], him[i], hre[j], him[j])
        spread(centers, halos, 2 * width * half)

    def finish(group, half):
        for u in range(width):
            p = first + group * width + u
            i, j = list_i[p], list_j[p]
            scale = 2.0 / (power[i] + power[j])
            slot = 2 * (width * half + u)
            re, im = gather(slot) * scale, gather(slot + 1) * scale
            cre[p] = re
            cim[p] = im
            ri, rj, ii, ij = are[i], are[j], aim[i], aim[j]
            are[i] = ri + re
            are[j] = rj + re
            aim[i] = ii + im
            aim[j] = ij - im

    def two(q, carry):
        multiply(2 * q + 1, 1)
        finish(2 * q, 0)
        multiply(2 * q + 2, 0)
        finish(2 * q + 1, 1)
        return carry

    multiply(0, 0)
    lax.fori_loop(0, (count + 2 * width - 1) // (2 * width), two, 0)


def groups(first, count, width, body):
    def one(q, carry):
        body(first + q * width)
        return carry

    lax.fori_loop(0, (count + width - 1) // width, one, 0)


def near_kernel(
    list_i, list_j, counts, band_ref, mine_ref, mate_ref, edge_mine_ref, edge_mate_ref,
    sre, sim, hre, him, power, are, aim, cre, cim, stage, *, dates, batch, width,
):
    _, rows, cols = sre.shape
    odd, _, _ = place()
    stage[...] = jnp.zeros_like(stage)
    boxes = make_boxes(rows, stage, band_ref)
    fields = (sre, sim, hre, him, power)
    load = loader(dates, cols, width, boxes, fields)
    load(mine_ref, 0, edge_mine_ref[...], (3 + odd) * dates)
    load(mate_ref, 0, edge_mate_ref[...], (4 - odd) * dates)
    are[...] = jnp.ones_like(are)
    aim[...] = jnp.zeros_like(aim)
    cohere(boxes, fields, (are, aim), list_i, list_j, cre, cim, 0, counts[0], batch)


def link_kernel(
    list_i, list_j, second, third, counts, band_ref, cross_ref, za_ref, zb_ref, *refs,
    batch, unroll, width, local_cap,
):
    out_ref, sre, sim, hre, him, power, are, aim, cre, cim, bre, bim, stage = refs[9:]
    _, dates, rows, cols = out_ref.shape
    tiles = 2 * dates + 1
    odd, far, _ = place()
    own = (3 + odd) * dates
    stage[...] = jnp.zeros_like(stage)
    boxes = make_boxes(rows, stage, band_ref)
    fields = (sre, sim, hre, him, power)
    load = loader(dates, cols, width, boxes, fields)
    others, n2, n3 = counts[1], counts[2], counts[3]

    load(cross_ref, 0, cross_ref[tiles - 1], 7 * odd * dates)
    up, down = 5 - 4 * far, 1 + 4 * far
    load(za_ref, 0, za_ref[tiles - 1], (up + odd) * dates)
    load(za_ref, tiles, za_ref[2 * tiles - 1], (up + 1 - odd) * dates)
    load(zb_ref, 0, zb_ref[tiles - 1], (down + odd) * dates)
    load(zb_ref, tiles, zb_ref[2 * tiles - 1], (down + 1 - odd) * dates)
    cohere(boxes, fields, (are, aim), list_i, list_j, cre, cim, local_cap, others, batch)

    def scaled(re, im):
        scale = lax.rsqrt(jnp.maximum(re * re + im * im, 1.0))
        return re * scale, im * scale

    def settle(low, count, xr, xi, yr, yi):
        def one(q, carry):
            for u in range(width):
                w = low + width * q + u
                re, im = scaled(xr[w], xi[w])
                xr[w] = re
                xi[w] = im
                yr[w] = re
                yi[w] = im
            return carry

        lax.fori_loop(0, count // width, one, 0)

    def step(index, count, xr, xi, yr, yi):
        def several(first):
            for u in range(unroll):
                p = index[first + u]
                i, j = list_i[p], list_j[p]
                re, im = cre[p], cim[p]
                nr, ni, fr, fi = xr[i], xi[i], xr[j], xi[j]
                ri, rj, ii, ij = yr[i], yr[j], yi[i], yi[j]
                yr[i] = ri + (re * fr - im * fi)
                yr[j] = rj + (re * nr + im * ni)
                yi[i] = ii + (re * fi + im * fr)
                yi[j] = ij + (re * ni - im * nr)

        groups(0, count, unroll, several)

    settle(own - 2 * dates, 5 * dates, are, aim, bre, bim)
    step(second, n2, are, aim, bre, bim)
    settle(own - dates, 3 * dates, bre, bim, are, aim)
    step(third, n3, bre, bim, are, aim)
    for k in range(dates):
        re, im = scaled(are[own + k], aim[own + k])
        out_ref[0, k] = re
        out_ref[1, k] = im


def swap(array, axis, matching):
    return lax.ppermute(array, axis, [*matching, *((j, i) for i, j in matching)])


def on_device(slc, pairs):
    comps, dates, rows, cols = slc.shape
    size = lax.axis_size("date")
    pair_count = pairs.shape[0]
    assert lax.axis_size("pix") == 2 and size % 2 == 0 and cols == LANES
    assert GAP <= dates and dates % 2 == 0 and comps * dates * WIN <= cols and rows % 8 == 0

    vmem = pl.BlockSpec(memory_space=pltpu.VMEM)
    smem = pl.BlockSpec(memory_space=pltpu.SMEM)

    def held(array):
        return pltpu.with_memory_space_constraint(array, pltpu.VMEM)

    def matching(step, keep):
        return [(i, i + step) for i in range(size - step) if keep(i)]

    main = slc.reshape(comps * dates, rows, cols)
    mates = matching(1, lambda i: i % 2 == 0)
    mate = swap(main, "date", mates)
    near, edge = pl.pallas_call(
        pack_edges,
        out_shape=[pltpu.VMEM(main.shape, slc.dtype), pltpu.VMEM((rows, cols), slc.dtype)],
        in_specs=[vmem],
        out_specs=[vmem] * 2,
    )(main)
    edge_mine = swap(edge, "pix", [(0, 1)])
    edge_mate = swap(edge, ("date", "pix"), [(2 * i + p, 2 * j + 1 - p) for i, j in mates for p in (0, 1)])
    cross = jnp.concatenate([near, edge_mine[None]], axis=0)
    both = jnp.concatenate([cross, mate, edge_mate[None]], axis=0)
    cross = swap(cross, "date", matching(3, lambda i: i % 2 == 1))
    za = swap(both, "date", matching(2, lambda i: i // 2 % 2 == 0))
    zb = swap(both, "date", matching(2, lambda i: i // 2 % 2 == 1))

    unroll = max(1, 128 // rows)
    batch = max(1, 128 // rows)
    width = max(w for w in range(1, 2 * unroll + 1) if dates % w == 0)
    per_block = min(pair_count, 2 * pair_count // size)
    local_cap = min(pair_count, 2 * per_block) + SPARE * unroll
    cap = local_cap + min(pair_count, 6 * per_block) + SPARE * unroll
    window = 8 * dates + 1
    stage = pltpu.VMEM((16 + max(width, 4 * batch) * (rows + 8), cols), jnp.float32)
    plane = 4 * rows * cols
    spare = 4 * 1024 * 1024 + 64 * plane
    lists = pl.pallas_call(
        functools.partial(select_kernel, dates=dates, unroll=unroll, local_cap=local_cap),
        out_shape=[pltpu.SMEM((n,), jnp.int32) for n in (cap, cap, pair_count + unroll, pair_count + unroll, 4)]
        + [pltpu.VMEM((2 * cols, cols), jnp.bfloat16)],
        in_specs=[smem],
        out_specs=[smem] * 5 + [vmem],
    )(pairs.T)
    band = held(lists[5])
    lists = [pltpu.with_memory_space_constraint(v, pltpu.SMEM) for v in lists[:5]]
    fields = [pltpu.VMEM((window, rows, cols), jnp.float32)] * 7 + [pltpu.VMEM((cap, rows, cols), jnp.float32)] * 2
    local = pl.pallas_call(
        functools.partial(near_kernel, dates=dates, batch=batch, width=width),
        out_shape=fields,
        in_specs=[smem] * 3 + [vmem] * 5,
        out_specs=[vmem] * 9,
        scratch_shapes=[stage],
        compiler_params=pltpu.CompilerParams(vmem_limit_bytes=spare),
    )(lists[0], lists[1], lists[4], band, held(near), held(mate), held(edge_mine), held(edge_mate))
    linked = pl.pallas_call(
        functools.partial(link_kernel, batch=batch, unroll=unroll, width=width, local_cap=local_cap),
        out_shape=[jax.ShapeDtypeStruct((comps, dates, rows, cols), jnp.float32), *fields],
        in_specs=[smem] * 5 + [vmem] * 13,
        out_specs=[vmem] * 10,
        input_output_aliases={9 + k: 1 + k for k in range(9)},
        scratch_shapes=[fields[0]] * 2 + [stage],
        compiler_params=pltpu.CompilerParams(vmem_limit_bytes=spare + 2 * window * plane),
    )(*lists, band, held(cross), held(za), held(zb), *(held(v) for v in local))
    return linked[0]


def solution(mesh):
    in_specs = (P(None, ("grp", "date"), None, "pix"), P("grp", None))
    out_specs = P(None, ("grp", "date"), None, "pix")

    return jax.shard_map(
        on_device, mesh=mesh, in_specs=in_specs, out_specs=out_specs, check_vma=False
    )
```

```python
import functools

import jax
import jax.numpy as jnp
from jax import lax
from jax.experimental import pallas as pl
from jax.experimental.pallas import tpu as pltpu
from jax.sharding import PartitionSpec as P


WIN = 2
GAP = 10
LANES = 128
SPARE = 3


def pack_edges(slc_ref, near_ref, edge_ref):
    tiles, rows, cols = slc_ref.shape
    lead = (1 - lax.axis_index("pix")) * WIN
    lane = lax.broadcasted_iota(jnp.int32, (rows, cols), 1)
    acc = jnp.zeros((rows, cols), jnp.float32)
    for t in range(tiles):
        moved = pltpu.roll(slc_ref[t].astype(jnp.float32), lead + WIN * t, 1)
        acc = jnp.where((lane >= WIN * t) & (lane < WIN * (t + 1)), moved, acc)
    near_ref[...] = slc_ref[...]
    edge_ref[...] = acc.astype(edge_ref.dtype)


def place():
    block = lax.axis_index("date")
    return block % 2, (block // 2) % 2, block // 2


def select_kernel(pairs_ref, list_i, list_j, second, third, counts, band_ref, *, dates, unroll, local_cap):
    cols = band_ref.shape[1]
    odd, _, chip = place()
    base = dates * (2 * chip - 3)
    own = base + (3 + odd) * dates
    inner = base + 3 * dates
    row = lax.broadcasted_iota(jnp.int32, band_ref.shape, 0)
    column = lax.broadcasted_iota(jnp.int32, band_ref.shape, 1)
    apart = jnp.where(row < cols, row, row - 2 * cols * lax.axis_index("pix")) - column
    band_ref[...] = jnp.where((apart <= WIN) & (apart >= -WIN), 1.0, 0.0).astype(band_ref.dtype)

    def one(p, found):
        near, other, n2, n3 = found
        i, j = pairs_ref[0, p], pairs_ref[1, p]

        def within(low, high):
            return ((j >= low) & (i < high)).astype(jnp.int32)

        local = ((i >= inner) & (j < inner + 2 * dates)).astype(jnp.int32)
        where = jnp.where(local == 1, near, other)
        list_i[where] = i - base
        list_j[where] = j - base
        second[n2] = where
        third[n3] = where
        return (
            near + local,
            other + (1 - local) * within(own - 2 * dates, own + 3 * dates),
            n2 + within(own - dates, own + 2 * dates),
            n3 + within(own, own + dates),
        )

    def four(q, found):
        for u in range(4):
            found = one(4 * q + u, found)
        return found

    zero = jnp.int32(0)
    total = pairs_ref.shape[1]
    found = (zero, jnp.int32(local_cap), zero, zero)
    found = lax.fori_loop(0, total // 4, four, found)
    near, other, n2, n3 = lax.fori_loop(total // 4 * 4, total, one, found)
    for u in range(SPARE * unroll):
        list_i[near + u] = 8 * dates
        list_j[near + u] = 8 * dates
        list_i[other + u] = 8 * dates
        list_j[other + u] = 8 * dates
    for u in range(unroll):
        second[n2 + u] = other
        third[n3 + u] = other
    counts[0] = near
    counts[1] = other - local_cap
    counts[2] = n2
    counts[3] = n3


def make_boxes(rows, stage, band_ref):
    pitch = rows + 8

    def spread(centers, halos, slot):
        values = jnp.concatenate([jnp.concatenate(centers, axis=0), jnp.concatenate(halos, axis=0)], axis=1)
        high = values.astype(jnp.bfloat16)
        low = (values - high.astype(jnp.float32)).astype(jnp.bfloat16)
        band = band_ref[...]
        wide = jnp.dot(high, band, preferred_element_type=jnp.float32)
        wide = wide + jnp.dot(low, band, preferred_element_type=jnp.float32)
        for k in range(len(centers)):
            stage[pl.ds(8 + (slot + k) * pitch, rows), :] = wide[k * rows : (k + 1) * rows]

    def gather(slot):
        start = 8 + slot * pitch
        result = stage[pl.ds(start, rows), :]
        for shift in range(1, WIN + 1):
            result = result + stage[pl.ds(start - shift, rows), :]
            result = result + stage[pl.ds(start + shift, rows), :]
        return result

    return spread, gather


def loader(dates, cols, width, boxes, fields):
    sre, sim, hre, him, power = fields
    spread, gather = boxes
    pix = lax.axis_index("pix")

    def load(ref, first, edge, target):
        edge = pltpu.roll(edge.astype(jnp.float32), -WIN * pix & (cols - 1), 1)
        for start in range(0, dates, width):
            squares, rims = [], []
            for k in range(start, start + width):
                re = ref[first + k].astype(jnp.float32)
                im = ref[first + dates + k].astype(jnp.float32)
                hr = pltpu.roll(edge, -WIN * k & (cols - 1), 1)
                hi = pltpu.roll(edge, -WIN * (dates + k) & (cols - 1), 1)
                sre[target + k] = re
                sim[target + k] = im
                hre[target + k] = hr
                him[target + k] = hi
                squares.append(re * re + im * im)
                rims.append(hr * hr + hi * hi)
            spread(squares, rims, 0)
            for u in range(width):
                power[target + start + u] = gather(u)

    return load


def cohere(boxes, fields, sums, list_i, list_j, cre, cim, first, count, width):
    sre, sim, hre, him, power = fields
    are, aim = sums
    spread, gather = boxes

    def cross(fr, fi, sr, si):
        return [fr * sr + fi * si, fi * sr - fr * si]

    def multiply(group, half):
        centers, halos = [], []
        for u in range(width):
            p = first + group * width + u
            i, j = list_i[p], list_j[p]
            centers += cross(sre[i], sim[i], sre[j], sim[j])
            halos += cross(hre[i], him[i], hre[j], him[j])
        spread(centers, halos, 2 * width * half)

    def finish(group, half):
        for u in range(width):
            p = first + group * width + u
            i, j = list_i[p], list_j[p]
            scale = 2.0 / (power[i] + power[j])
            slot = 2 * (width * half + u)
            re, im = gather(slot) * scale, gather(slot + 1) * scale
            cre[p] = re
            cim[p] = im
            ri, rj, ii, ij = are[i], are[j], aim[i], aim[j]
            are[i] = ri + re
            are[j] = rj + re
            aim[i] = ii + im
            aim[j] = ij - im

    def two(q, carry):
        multiply(2 * q + 1, 1)
        finish(2 * q, 0)
        multiply(2 * q + 2, 0)
        finish(2 * q + 1, 1)
        return carry

    multiply(0, 0)
    lax.fori_loop(0, (count + 2 * width - 1) // (2 * width), two, 0)


def groups(first, count, width, body):
    def one(q, carry):
        body(first + q * width)
        return carry

    lax.fori_loop(0, (count + width - 1) // width, one, 0)


def near_kernel(
    list_i, list_j, counts, band_ref, mine_ref, mate_ref, edge_mine_ref, edge_mate_ref,
    sre, sim, hre, him, power, are, aim, cre, cim, stage, *, dates, batch, width,
):
    _, rows, cols = sre.shape
    odd, _, _ = place()
    stage[...] = jnp.zeros_like(stage)
    boxes = make_boxes(rows, stage, band_ref)
    fields = (sre, sim, hre, him, power)
    load = loader(dates, cols, width, boxes, fields)
    load(mine_ref, 0, edge_mine_ref[...], (3 + odd) * dates)
    load(mate_ref, 0, edge_mate_ref[...], (4 - odd) * dates)
    are[...] = jnp.ones_like(are)
    aim[...] = jnp.zeros_like(aim)
    cohere(boxes, fields, (are, aim), list_i, list_j, cre, cim, 0, counts[0], batch)


def link_kernel(
    list_i, list_j, second, third, counts, band_ref, cross_ref, za_ref, zb_ref, *refs,
    batch, unroll, width, local_cap,
):
    out_ref, sre, sim, hre, him, power, are, aim, cre, cim, bre, bim, stage = refs[9:]
    _, dates, rows, cols = out_ref.shape
    tiles = 2 * dates + 1
    odd, far, _ = place()
    own = (3 + odd) * dates
    stage[...] = jnp.zeros_like(stage)
    boxes = make_boxes(rows, stage, band_ref)
    fields = (sre, sim, hre, him, power)
    load = loader(dates, cols, width, boxes, fields)
    others, n2, n3 = counts[1], counts[2], counts[3]

    load(cross_ref, 0, cross_ref[tiles - 1], 7 * odd * dates)
    up, down = 5 - 4 * far, 1 + 4 * far
    load(za_ref, 0, za_ref[tiles - 1], (up + odd) * dates)
    load(za_ref, tiles, za_ref[2 * tiles - 1], (up + 1 - odd) * dates)
    load(zb_ref, 0, zb_ref[tiles - 1], (down + odd) * dates)
    load(zb_ref, tiles, zb_ref[2 * tiles - 1], (down + 1 - odd) * dates)
    cohere(boxes, fields, (are, aim), list_i, list_j, cre, cim, local_cap, others, batch)

    def scaled(re, im):
        scale = lax.rsqrt(jnp.maximum(re * re + im * im, 1.0))
        return re * scale, im * scale

    def settle(low, count, xr, xi, yr, yi):
        def one(q, carry):
            for u in range(width):
                w = low + width * q + u
                re, im = scaled(xr[w], xi[w])
                xr[w] = re
                xi[w] = im
                yr[w] = re
                yi[w] = im
            return carry

        lax.fori_loop(0, count // width, one, 0)

    def step(index, count, xr, xi, yr, yi):
        def several(first):
            for u in range(unroll):
                p = index[first + u]
                i, j = list_i[p], list_j[p]
                re, im = cre[p], cim[p]
                nr, ni, fr, fi = xr[i], xi[i], xr[j], xi[j]
                ri, rj, ii, ij = yr[i], yr[j], yi[i], yi[j]
                yr[i] = ri + (re * fr - im * fi)
                yr[j] = rj + (re * nr + im * ni)
                yi[i] = ii + (re * fi + im * fr)
                yi[j] = ij + (re * ni - im * nr)

        groups(0, count, unroll, several)

    settle(own - 2 * dates, 5 * dates, are, aim, bre, bim)
    step(second, n2, are, aim, bre, bim)
    settle(own - dates, 3 * dates, bre, bim, are, aim)
    step(third, n3, bre, bim, are, aim)
    for k in range(dates):
        re, im = scaled(are[own + k], aim[own + k])
        out_ref[0, k] = re
        out_ref[1, k] = im


def swap(array, axis, matching):
    matched = {i for pair in matching for i in pair}
    alone = [i for i in range(lax.axis_size(axis)) if i not in matched]
    pairing = [*matching, *zip(alone[::2], alone[1::2], strict=True)]
    return lax.ppermute(array, axis, [*pairing, *((j, i) for i, j in pairing)])


def on_device(slc, pairs):
    comps, dates, rows, cols = slc.shape
    size = lax.axis_size("date")
    pair_count = pairs.shape[0]
    assert lax.axis_size("pix") == 2 and size % 2 == 0 and cols == LANES
    assert GAP <= dates and dates % 2 == 0 and comps * dates * WIN <= cols and rows % 8 == 0

    vmem = pl.BlockSpec(memory_space=pltpu.VMEM)
    smem = pl.BlockSpec(memory_space=pltpu.SMEM)

    def held(array):
        return pltpu.with_memory_space_constraint(array, pltpu.VMEM)

    def matching(step, keep):
        return [(i, i + step) for i in range(size - step) if keep(i)]

    main = slc.reshape(comps * dates, rows, cols)
    mates = matching(1, lambda i: i % 2 == 0)
    mate = swap(main, "date", mates)
    near, edge = pl.pallas_call(
        pack_edges,
        out_shape=[pltpu.VMEM(main.shape, slc.dtype), pltpu.VMEM((rows, cols), slc.dtype)],
        in_specs=[vmem],
        out_specs=[vmem] * 2,
    )(main)
    edge_mine = swap(edge, "pix", [(0, 1)])
    edge_mate = swap(edge, ("date", "pix"), [(2 * i + p, 2 * j + 1 - p) for i, j in mates for p in (0, 1)])
    cross = jnp.concatenate([near, edge_mine[None]], axis=0)
    both = jnp.concatenate([cross, mate, edge_mate[None]], axis=0)
    cross = swap(cross, "date", matching(3, lambda i: i % 2 == 1))
    za = swap(both, "date", matching(2, lambda i: i // 2 % 2 == 0))
    zb = swap(both, "date", matching(2, lambda i: i // 2 % 2 == 1))

    unroll = max(1, 128 // rows)
    batch = max(1, 128 // rows)
    width = max(w for w in range(1, 2 * unroll + 1) if dates % w == 0)
    per_block = min(pair_count, 2 * pair_count // size)
    local_cap = min(pair_count, 2 * per_block) + SPARE * unroll
    cap = local_cap + min(pair_count, 6 * per_block) + SPARE * unroll
    window = 8 * dates + 1
    stage = pltpu.VMEM((16 + max(width, 4 * batch) * (rows + 8), cols), jnp.float32)
    plane = 4 * rows * cols
    spare = 4 * 1024 * 1024 + 64 * plane
    lists = pl.pallas_call(
        functools.partial(select_kernel, dates=dates, unroll=unroll, local_cap=local_cap),
        out_shape=[pltpu.SMEM((n,), jnp.int32) for n in (cap, cap, pair_count + unroll, pair_count + unroll, 4)]
        + [pltpu.VMEM((2 * cols, cols), jnp.bfloat16)],
        in_specs=[smem],
        out_specs=[smem] * 5 + [vmem],
    )(pairs.T)
    band = held(lists[5])
    lists = [pltpu.with_memory_space_constraint(v, pltpu.SMEM) for v in lists[:5]]
    fields = [pltpu.VMEM((window, rows, cols), jnp.float32)] * 7 + [pltpu.VMEM((cap, rows, cols), jnp.float32)] * 2
    local = pl.pallas_call(
        functools.partial(near_kernel, dates=dates, batch=batch, width=width),
        out_shape=fields,
        in_specs=[smem] * 3 + [vmem] * 5,
        out_specs=[vmem] * 9,
        scratch_shapes=[stage],
        compiler_params=pltpu.CompilerParams(vmem_limit_bytes=spare),
    )(lists[0], lists[1], lists[4], band, held(near), held(mate), held(edge_mine), held(edge_mate))
    linked = pl.pallas_call(
        functools.partial(link_kernel, batch=batch, unroll=unroll, width=width, local_cap=local_cap),
        out_shape=[jax.ShapeDtypeStruct((comps, dates, rows, cols), jnp.float32), *fields],
        in_specs=[smem] * 5 + [vmem] * 13,
        out_specs=[vmem] * 10,
        input_output_aliases={9 + k: 1 + k for k in range(9)},
        scratch_shapes=[fields[0]] * 2 + [stage],
        compiler_params=pltpu.CompilerParams(vmem_limit_bytes=spare + 2 * window * plane),
    )(*lists, band, held(cross), held(za), held(zb), *(held(v) for v in local))
    return linked[0]


def solution(mesh):
    in_specs = (P(None, ("grp", "date"), None, "pix"), P("grp", None))
    out_specs = P(None, ("grp", "date"), None, "pix")

    return jax.shard_map(
        on_device, mesh=mesh, in_specs=in_specs, out_specs=out_specs, check_vma=False
    )
```

```python
import functools

import jax
import jax.numpy as jnp
from jax import lax
from jax.experimental import pallas as pl
from jax.experimental.pallas import tpu as pltpu
from jax.sharding import PartitionSpec as P


WIN = 2
GAP = 10
LANES = 128
SPARE = 3


def pack_edges(slc_ref, near_ref, edge_ref):
    tiles, rows, cols = slc_ref.shape
    lead = (1 - lax.axis_index("pix")) * WIN
    lane = lax.broadcasted_iota(jnp.int32, (rows, cols), 1)
    acc = jnp.zeros((rows, cols), jnp.float32)
    for t in range(tiles):
        moved = pltpu.roll(slc_ref[t].astype(jnp.float32), lead + WIN * t, 1)
        acc = jnp.where((lane >= WIN * t) & (lane < WIN * (t + 1)), moved, acc)
    near_ref[...] = slc_ref[...]
    edge_ref[...] = acc.astype(edge_ref.dtype)


def place():
    block = lax.axis_index("date")
    return block % 2, (block // 2) % 2, block // 2


def select_kernel(
    pairs_ref, list_i, list_j, second, third, counts, band_ref, of_first, of_second,
    *, dates, size, unroll, mid_at, late_at,
):
    cols = band_ref.shape[1]
    odd, far, chip = place()
    base = dates * (2 * chip - 3)
    row = lax.broadcasted_iota(jnp.int32, band_ref.shape, 0)
    column = lax.broadcasted_iota(jnp.int32, band_ref.shape, 1)
    apart = jnp.where(row < cols, row, row - 2 * cols * lax.axis_index("pix")) - column
    band_ref[...] = jnp.where((apart <= WIN) & (apart >= -WIN), 1.0, 0.0).astype(band_ref.dtype)

    def classify(block, carry):
        slot = block - (2 * chip - 3)
        away = slot - 3 - odd
        near = jnp.where((slot == 3) | (slot == 4), 1, 0)
        soon = jnp.where((slot == 1 + 4 * far) | (slot == 2 + 4 * far), 0, 2)
        first = jnp.where(away <= 2, soon, 0) + near
        second = jnp.where(away >= -2, soon, 0) + near
        for reach in range(3):
            first = first + jnp.where(away <= reach, 16 >> reach, 0)
            second = second + jnp.where(away >= -reach, 16 >> reach, 0)
        for k in range(dates):
            of_first[block * dates + k] = first
            of_second[block * dates + k] = second
        return carry

    lax.fori_loop(0, size, classify, 0)

    def several(width):
        def run(q, found):
            at = [width * q + u for u in range(width)]
            ends = [(pairs_ref[0, p], pairs_ref[1, p]) for p in at]
            bits = [of_first[i] & of_second[j] for i, j in ends]
            near, mid, late, n2, n3 = found
            for (i, j), bit in zip(ends, bits, strict=True):
                here, soon = bit & 1, (bit >> 1) & 1
                where = jnp.where(here == 1, near, jnp.where(soon == 1, mid, late))
                list_i[where] = i - base
                list_j[where] = j - base
                second[n2] = where
                third[n3] = where
                near = near + here
                mid = mid + soon - here
                late = late + ((bit >> 2) & 1) - soon
                n2 = n2 + ((bit >> 3) & 1)
                n3 = n3 + (bit >> 4)
            return near, mid, late, n2, n3

        return run

    zero = jnp.int32(0)
    total = pairs_ref.shape[1]
    found = (zero, jnp.int32(mid_at), jnp.int32(late_at), zero, zero)
    found = lax.fori_loop(0, total // 8, several(8), found)
    near, mid, late, n2, n3 = lax.fori_loop(total // 8 * 8, total, several(1), found)
    for end in (near, mid, late):
        for u in range(SPARE * unroll):
            list_i[end + u] = 8 * dates
            list_j[end + u] = 8 * dates
    for u in range(unroll):
        second[n2 + u] = late
        third[n3 + u] = late
    counts[0] = near
    counts[1] = mid - mid_at
    counts[2] = late - late_at
    counts[3] = n2
    counts[4] = n3


def make_boxes(rows, stage, band_ref):
    pitch = rows + 8

    def spread(centers, halos, slot):
        values = jnp.concatenate([jnp.concatenate(centers, axis=0), jnp.concatenate(halos, axis=0)], axis=1)
        high = values.astype(jnp.bfloat16)
        low = (values - high.astype(jnp.float32)).astype(jnp.bfloat16)
        band = band_ref[...]
        wide = jnp.dot(high, band, preferred_element_type=jnp.float32)
        wide = wide + jnp.dot(low, band, preferred_element_type=jnp.float32)
        for k in range(len(centers)):
            stage[pl.ds(8 + (slot + k) * pitch, rows), :] = wide[k * rows : (k + 1) * rows]

    def gather(slot):
        start = 8 + slot * pitch
        result = stage[pl.ds(start, rows), :]
        for shift in range(1, WIN + 1):
            result = result + stage[pl.ds(start - shift, rows), :]
            result = result + stage[pl.ds(start + shift, rows), :]
        return result

    return spread, gather


def loader(dates, cols, width, boxes, fields):
    sre, sim, hre, him, power = fields
    spread, gather = boxes
    pix = lax.axis_index("pix")

    def load(ref, first, edge, target):
        edge = pltpu.roll(edge.astype(jnp.float32), -WIN * pix & (cols - 1), 1)
        for start in range(0, dates, width):
            squares, rims = [], []
            for k in range(start, start + width):
                re = ref[first + k].astype(jnp.float32)
                im = ref[first + dates + k].astype(jnp.float32)
                hr = pltpu.roll(edge, -WIN * k & (cols - 1), 1)
                hi = pltpu.roll(edge, -WIN * (dates + k) & (cols - 1), 1)
                sre[target + k] = re
                sim[target + k] = im
                hre[target + k] = hr
                him[target + k] = hi
                squares.append(re * re + im * im)
                rims.append(hr * hr + hi * hi)
            spread(squares, rims, 0)
            for u in range(width):
                power[target + start + u] = gather(u)

    return load


def cohere(boxes, fields, sums, list_i, list_j, cre, cim, first, count, width):
    sre, sim, hre, him, power = fields
    are, aim = sums
    spread, gather = boxes

    def cross(fr, fi, sr, si):
        return [fr * sr + fi * si, fi * sr - fr * si]

    def multiply(group, half):
        centers, halos = [], []
        for u in range(width):
            p = first + group * width + u
            i, j = list_i[p], list_j[p]
            centers += cross(sre[i], sim[i], sre[j], sim[j])
            halos += cross(hre[i], him[i], hre[j], him[j])
        spread(centers, halos, 2 * width * half)

    def finish(group, half):
        for u in range(width):
            p = first + group * width + u
            i, j = list_i[p], list_j[p]
            scale = 2.0 / (power[i] + power[j])
            slot = 2 * (width * half + u)
            re, im = gather(slot) * scale, gather(slot + 1) * scale
            cre[p] = re
            cim[p] = im
            ri, rj, ii, ij = are[i], are[j], aim[i], aim[j]
            are[i] = ri + re
            are[j] = rj + re
            aim[i] = ii + im
            aim[j] = ij - im

    def two(q, carry):
        multiply(2 * q + 1, 1)
        finish(2 * q, 0)
        multiply(2 * q + 2, 0)
        finish(2 * q + 1, 1)
        return carry

    multiply(0, 0)
    lax.fori_loop(0, (count + 2 * width - 1) // (2 * width), two, 0)


def groups(first, count, width, body):
    def one(q, carry):
        body(first + q * width)
        return carry

    lax.fori_loop(0, (count + width - 1) // width, one, 0)


def near_kernel(
    list_i, list_j, counts, band_ref, mine_ref, mate_ref, edge_mine_ref, edge_mate_ref,
    sre, sim, hre, him, power, are, aim, cre, cim, stage, *, dates, batch, width,
):
    _, rows, cols = sre.shape
    odd, _, _ = place()
    stage[...] = jnp.zeros_like(stage)
    boxes = make_boxes(rows, stage, band_ref)
    fields = (sre, sim, hre, him, power)
    load = loader(dates, cols, width, boxes, fields)
    load(mine_ref, 0, edge_mine_ref[...], (3 + odd) * dates)
    load(mate_ref, 0, edge_mate_ref[...], (4 - odd) * dates)
    are[...] = jnp.ones_like(are)
    aim[...] = jnp.zeros_like(aim)
    cohere(boxes, fields, (are, aim), list_i, list_j, cre, cim, 0, counts[0], batch)


def mid_kernel(list_i, list_j, counts, band_ref, cross_ref, za_ref, *refs, batch, width, dates, mid_at):
    sre, sim, hre, him, power, are, aim, cre, cim, stage = refs[9:]
    _, rows, cols = sre.shape
    tiles = 2 * dates + 1
    odd, far, _ = place()
    stage[...] = jnp.zeros_like(stage)
    boxes = make_boxes(rows, stage, band_ref)
    fields = (sre, sim, hre, him, power)
    load = loader(dates, cols, width, boxes, fields)
    up = 5 - 4 * far
    load(cross_ref, 0, cross_ref[tiles - 1], 7 * odd * dates)
    load(za_ref, 0, za_ref[tiles - 1], (up + odd) * dates)
    load(za_ref, tiles, za_ref[2 * tiles - 1], (up + 1 - odd) * dates)
    cohere(boxes, fields, (are, aim), list_i, list_j, cre, cim, mid_at, counts[1], batch)


def link_kernel(
    list_i, list_j, second, third, counts, band_ref, zb_ref, *refs,
    batch, unroll, width, late_at,
):
    out_ref, sre, sim, hre, him, power, are, aim, cre, cim, bre, bim, stage = refs[9:]
    _, dates, rows, cols = out_ref.shape
    tiles = 2 * dates + 1
    odd, far, _ = place()
    own = (3 + odd) * dates
    stage[...] = jnp.zeros_like(stage)
    boxes = make_boxes(rows, stage, band_ref)
    fields = (sre, sim, hre, him, power)
    load = loader(dates, cols, width, boxes, fields)
    others, n2, n3 = counts[2], counts[3], counts[4]
    down = 1 + 4 * far
    load(zb_ref, 0, zb_ref[tiles - 1], (down + odd) * dates)
    load(zb_ref, tiles, zb_ref[2 * tiles - 1], (down + 1 - odd) * dates)
    cohere(boxes, fields, (are, aim), list_i, list_j, cre, cim, late_at, others, batch)

    def scaled(re, im):
        scale = lax.rsqrt(jnp.maximum(re * re + im * im, 1.0))
        return re * scale, im * scale

    def settle(low, count, xr, xi, yr, yi):
        def one(q, carry):
            for u in range(width):
                w = low + width * q + u
                re, im = scaled(xr[w], xi[w])
                xr[w] = re
                xi[w] = im
                yr[w] = re
                yi[w] = im
            return carry

        lax.fori_loop(0, count // width, one, 0)

    def step(index, count, xr, xi, yr, yi):
        def several(first):
            for u in range(unroll):
                p = index[first + u]
                i, j = list_i[p], list_j[p]
                re, im = cre[p], cim[p]
                nr, ni, fr, fi = xr[i], xi[i], xr[j], xi[j]
                ri, rj, ii, ij = yr[i], yr[j], yi[i], yi[j]
                yr[i] = ri + (re * fr - im * fi)
                yr[j] = rj + (re * nr + im * ni)
                yi[i] = ii + (re * fi + im * fr)
                yi[j] = ij + (re * ni - im * nr)

        groups(0, count, unroll, several)

    settle(own - 2 * dates, 5 * dates, are, aim, bre, bim)
    step(second, n2, are, aim, bre, bim)
    settle(own - dates, 3 * dates, bre, bim, are, aim)
    step(third, n3, bre, bim, are, aim)
    for k in range(dates):
        re, im = scaled(are[own + k], aim[own + k])
        out_ref[0, k] = re
        out_ref[1, k] = im


def swap(array, axis, matching):
    matched = {i for pair in matching for i in pair}
    alone = [i for i in range(lax.axis_size(axis)) if i not in matched]
    pairing = [*matching, *zip(alone[::2], alone[1::2], strict=True)]
    return lax.ppermute(array, axis, [*pairing, *((j, i) for i, j in pairing)])


def on_device(slc, pairs):
    comps, dates, rows, cols = slc.shape
    size = lax.axis_size("date")
    pair_count = pairs.shape[0]
    assert lax.axis_size("pix") == 2 and size % 2 == 0 and cols == LANES
    assert GAP <= dates and dates % 2 == 0 and comps * dates * WIN <= cols and rows % 8 == 0

    vmem = pl.BlockSpec(memory_space=pltpu.VMEM)
    smem = pl.BlockSpec(memory_space=pltpu.SMEM)

    def held(array):
        return pltpu.with_memory_space_constraint(array, pltpu.VMEM)

    def matching(step, keep):
        return [(i, i + step) for i in range(size - step) if keep(i)]

    small = pltpu.CompilerParams(vmem_limit_bytes=4 * 1024 * 1024)
    main = slc.reshape(comps * dates, rows, cols)
    mates = matching(1, lambda i: i % 2 == 0)
    mate = swap(main, "date", mates)
    near, edge = pl.pallas_call(
        pack_edges,
        out_shape=[pltpu.VMEM(main.shape, slc.dtype), pltpu.VMEM((rows, cols), slc.dtype)],
        in_specs=[vmem],
        out_specs=[vmem] * 2,
        compiler_params=small,
    )(main)
    edge_mine = swap(edge, "pix", [(0, 1)])
    edge_mate = swap(edge, ("date", "pix"), [(2 * i + p, 2 * j + 1 - p) for i, j in mates for p in (0, 1)])
    cross = jnp.concatenate([near, edge_mine[None]], axis=0)
    both = jnp.concatenate([cross, mate, edge_mate[None]], axis=0)
    cross = swap(cross, "date", matching(3, lambda i: i % 2 == 1))
    za = swap(both, "date", matching(2, lambda i: i // 2 % 2 == 0))
    zb = swap(both, "date", matching(2, lambda i: i // 2 % 2 == 1))

    unroll = max(1, 128 // rows)
    batch = max(1, 128 // rows)
    width = max(w for w in range(1, 2 * unroll + 1) if dates % w == 0)
    per_block = min(pair_count, 2 * pair_count // size)
    mid_at = min(pair_count, 2 * per_block) + SPARE * unroll
    late_at = mid_at + min(pair_count, 4 * per_block) + SPARE * unroll
    cap = late_at + min(pair_count, 4 * per_block) + SPARE * unroll
    window = 8 * dates + 1
    stage = pltpu.VMEM((16 + max(width, 4 * batch) * (rows + 8), cols), jnp.float32)
    plane = 4 * rows * cols
    spare = 4 * 1024 * 1024 + 64 * plane
    chosen = pl.pallas_call(
        functools.partial(
            select_kernel, dates=dates, size=size, unroll=unroll, mid_at=mid_at, late_at=late_at
        ),
        out_shape=[pltpu.SMEM((n,), jnp.int32) for n in (cap, cap, pair_count + unroll, pair_count + unroll, 5)]
        + [pltpu.VMEM((2 * cols, cols), jnp.bfloat16)],
        in_specs=[smem],
        out_specs=[smem] * 5 + [vmem],
        scratch_shapes=[pltpu.SMEM((size * dates,), jnp.int32)] * 2,
        compiler_params=small,
    )
    lists = chosen(pairs.T)
    band = held(lists[5])
    lists = [pltpu.with_memory_space_constraint(v, pltpu.SMEM) for v in lists[:5]]
    fields = [pltpu.VMEM((window, rows, cols), jnp.float32)] * 7 + [pltpu.VMEM((cap, rows, cols), jnp.float32)] * 2
    local = pl.pallas_call(
        functools.partial(near_kernel, dates=dates, batch=batch, width=width),
        out_shape=fields,
        in_specs=[smem] * 3 + [vmem] * 5,
        out_specs=[vmem] * 9,
        scratch_shapes=[stage],
        compiler_params=pltpu.CompilerParams(vmem_limit_bytes=spare),
    )(lists[0], lists[1], lists[4], band, held(near), held(mate), held(edge_mine), held(edge_mate))
    local = pl.pallas_call(
        functools.partial(mid_kernel, batch=batch, width=width, dates=dates, mid_at=mid_at),
        out_shape=fields,
        in_specs=[smem] * 3 + [vmem] * 12,
        out_specs=[vmem] * 9,
        input_output_aliases={6 + k: k for k in range(9)},
        scratch_shapes=[stage],
        compiler_params=pltpu.CompilerParams(vmem_limit_bytes=spare),
    )(lists[0], lists[1], lists[4], band, held(cross), held(za), *(held(v) for v in local))
    linked = pl.pallas_call(
        functools.partial(link_kernel, batch=batch, unroll=unroll, width=width, late_at=late_at),
        out_shape=[jax.ShapeDtypeStruct((comps, dates, rows, cols), jnp.float32), *fields],
        in_specs=[smem] * 5 + [vmem] * 11,
        out_specs=[vmem] * 10,
        input_output_aliases={7 + k: 1 + k for k in range(9)},
        scratch_shapes=[fields[0]] * 2 + [stage],
        compiler_params=pltpu.CompilerParams(vmem_limit_bytes=spare + 2 * window * plane),
    )(*lists, band, held(zb), *(held(v) for v in local))
    return linked[0]


def solution(mesh):
    in_specs = (P(None, ("grp", "date"), None, "pix"), P("grp", None))
    out_specs = P(None, ("grp", "date"), None, "pix")

    return jax.shard_map(
        on_device, mesh=mesh, in_specs=in_specs, out_specs=out_specs, check_vma=False
    )
```

```python
import functools

import jax
import jax.numpy as jnp
from jax import lax
from jax.experimental import pallas as pl
from jax.experimental.pallas import tpu as pltpu
from jax.sharding import PartitionSpec as P


WIN = 2
GAP = 10
LANES = 128
SPARE = 3


def pack_edges(slc_ref, near_ref, edge_ref):
    tiles, rows, cols = slc_ref.shape
    lead = (1 - lax.axis_index("pix")) * WIN
    lane = lax.broadcasted_iota(jnp.int32, (rows, cols), 1)
    acc = jnp.zeros((rows, cols), jnp.float32)
    for t in range(tiles):
        moved = pltpu.roll(slc_ref[t].astype(jnp.float32), lead + WIN * t, 1)
        acc = jnp.where((lane >= WIN * t) & (lane < WIN * (t + 1)), moved, acc)
    near_ref[...] = slc_ref[...]
    edge_ref[...] = acc.astype(edge_ref.dtype)


def place():
    block = lax.axis_index("date")
    return block % 2, (block // 2) % 2, block // 2


def select_kernel(pairs_ref, *refs, dates, mid_at, late_at, cap):
    outs, band_ref, padded, staged, sems = refs[:5], refs[5], refs[6], refs[7:12], refs[12]
    cols = band_ref.shape[1]
    odd, far, chip = place()
    own, inner, last = (3 + odd) * dates, 3 * dates, (1 + 4 * far) * dates
    row = lax.broadcasted_iota(jnp.int32, band_ref.shape, 0)
    column = lax.broadcasted_iota(jnp.int32, band_ref.shape, 1)
    apart = jnp.where(row < cols, row, row - 2 * cols * lax.axis_index("pix")) - column
    band_ref[...] = jnp.where((apart <= WIN) & (apart >= -WIN), 1.0, 0.0).astype(band_ref.dtype)

    lanes, length = padded.shape[1], staged[0].shape[1]
    padded[...] = jnp.full(padded.shape, -(2**20), jnp.int32)
    padded[pl.ds(0, 2), pl.ds(0, pairs_ref.shape[1])] = pairs_ref[...]
    dated = padded[...] - dates * (2 * chip - 3)
    i, j = dated[0:1], dated[1:2]

    def flag(condition):
        return jnp.where(condition, 1.0, 0.0)

    def within(reach):
        return flag(j >= own - reach * dates) * flag(i < own + (reach + 1) * dates)

    def absent(date):
        return 1.0 - flag(date >= last) * flag(date < last + 2 * dates)

    near = flag(i >= inner) * flag(j < inner + 2 * dates)
    wanted = within(2)
    soon = wanted * absent(i) * absent(j)
    classes = [near, soon - near, wanted - soon, within(1), within(0)]
    empty = jnp.zeros((1, lanes), jnp.float32)
    stack = jnp.concatenate([*classes, empty, empty, empty], axis=0)
    before = flag(
        lax.broadcasted_iota(jnp.int32, (lanes, lanes), 0) < lax.broadcasted_iota(jnp.int32, (lanes, lanes), 1)
    ).astype(jnp.bfloat16)
    ranks = jnp.dot(stack.astype(jnp.bfloat16), before, preferred_element_type=jnp.float32)
    rank = [ranks[k : k + 1] for k in range(5)]
    where = classes[0] * rank[0] + classes[1] * (rank[1] + mid_at) + classes[2] * (rank[2] + late_at)
    targets = [where + wanted - 1.0, classes[3] * (rank[3] + 1.0) - 1.0, classes[4] * (rank[4] + 1.0) - 1.0]
    upright = jnp.transpose(jnp.concatenate([*targets, *[empty] * 5], axis=0))
    slots = lax.broadcasted_iota(jnp.int32, (lanes, length), 1).astype(jnp.float32)
    ones = jnp.ones((1, lanes), jnp.float32)
    upper = jnp.floor(where * (1.0 / 128.0))

    def scatter(k, values):
        hot = flag(upright[:, k : k + 1] == slots).astype(jnp.bfloat16)
        rows = jnp.concatenate([*values, *[empty] * (8 - len(values))], axis=0).astype(jnp.bfloat16)
        return jnp.dot(rows, hot, preferred_element_type=jnp.float32)

    ends = scatter(0, [i.astype(jnp.float32) * wanted, j.astype(jnp.float32) * wanted, ones])
    free = 8.0 * dates * (1.0 - ends[2:3])
    staged[0][...] = (ends[0:1] + free).astype(jnp.int32)
    staged[1][...] = (ends[1:2] + free).astype(jnp.int32)
    for k in (1, 2):
        index = scatter(k, [upper, where - 128.0 * upper, ones])
        spot = 128.0 * index[0:1] + index[1:2] + (cap - 1.0) * (1.0 - index[2:3])
        staged[1 + k][...] = spot.astype(jnp.int32)
    sums = jnp.broadcast_to(jnp.sum(stack, axis=1, keepdims=True), (8, length))
    own_lane = flag(
        lax.broadcasted_iota(jnp.int32, (8, length), 0) == lax.broadcasted_iota(jnp.int32, (8, length), 1)
    )
    staged[4][...] = jnp.sum(sums * own_lane, axis=0, keepdims=True).astype(jnp.int32)
    copies = [pltpu.make_async_copy(staged[k], outs[k], sems.at[k]) for k in range(5)]
    for copy in copies:
        copy.start()
    for copy in copies:
        copy.wait()


def make_boxes(rows, stage, band_ref):
    pitch = rows + 8

    def spread(centers, halos, slot):
        values = jnp.concatenate([jnp.concatenate(centers, axis=0), jnp.concatenate(halos, axis=0)], axis=1)
        high = values.astype(jnp.bfloat16)
        low = (values - high.astype(jnp.float32)).astype(jnp.bfloat16)
        band = band_ref[...]
        wide = jnp.dot(high, band, preferred_element_type=jnp.float32)
        wide = wide + jnp.dot(low, band, preferred_element_type=jnp.float32)
        for k in range(len(centers)):
            stage[pl.ds(8 + (slot + k) * pitch, rows), :] = wide[k * rows : (k + 1) * rows]

    def gather(slot):
        start = 8 + slot * pitch
        result = stage[pl.ds(start, rows), :]
        for shift in range(1, WIN + 1):
            result = result + stage[pl.ds(start - shift, rows), :]
            result = result + stage[pl.ds(start + shift, rows), :]
        return result

    return spread, gather


def loader(dates, cols, width, boxes, fields):
    sre, sim, hre, him, power = fields
    spread, gather = boxes
    pix = lax.axis_index("pix")

    def load(ref, first, edge, target):
        edge = pltpu.roll(edge.astype(jnp.float32), -WIN * pix & (cols - 1), 1)
        for start in range(0, dates, width):
            squares, rims = [], []
            for k in range(start, start + width):
                re = ref[first + k].astype(jnp.float32)
                im = ref[first + dates + k].astype(jnp.float32)
                hr = pltpu.roll(edge, -WIN * k & (cols - 1), 1)
                hi = pltpu.roll(edge, -WIN * (dates + k) & (cols - 1), 1)
                sre[target + k] = re
                sim[target + k] = im
                hre[target + k] = hr
                him[target + k] = hi
                squares.append(re * re + im * im)
                rims.append(hr * hr + hi * hi)
            spread(squares, rims, 0)
            for u in range(width):
                power[target + start + u] = gather(u)

    return load


def cohere(boxes, fields, sums, list_i, list_j, cre, cim, first, count, width):
    sre, sim, hre, him, power = fields
    are, aim = sums
    spread, gather = boxes

    def cross(fr, fi, sr, si):
        return [fr * sr + fi * si, fi * sr - fr * si]

    def multiply(group, half):
        centers, halos = [], []
        for u in range(width):
            p = first + group * width + u
            i, j = list_i[0, p], list_j[0, p]
            centers += cross(sre[i], sim[i], sre[j], sim[j])
            halos += cross(hre[i], him[i], hre[j], him[j])
        spread(centers, halos, 2 * width * half)

    def finish(group, half):
        for u in range(width):
            p = first + group * width + u
            i, j = list_i[0, p], list_j[0, p]
            scale = 2.0 / (power[i] + power[j])
            slot = 2 * (width * half + u)
            re, im = gather(slot) * scale, gather(slot + 1) * scale
            cre[p] = re
            cim[p] = im
            ri, rj, ii, ij = are[i], are[j], aim[i], aim[j]
            are[i] = ri + re
            are[j] = rj + re
            aim[i] = ii + im
            aim[j] = ij - im

    def two(q, carry):
        multiply(2 * q + 1, 1)
        finish(2 * q, 0)
        multiply(2 * q + 2, 0)
        finish(2 * q + 1, 1)
        return carry

    multiply(0, 0)
    lax.fori_loop(0, (count + 2 * width - 1) // (2 * width), two, 0)


def groups(first, count, width, body):
    def one(q, carry):
        body(first + q * width)
        return carry

    lax.fori_loop(0, (count + width - 1) // width, one, 0)


def near_kernel(
    list_i, list_j, counts, band_ref, mine_ref, mate_ref, edge_mine_ref, edge_mate_ref,
    sre, sim, hre, him, power, are, aim, cre, cim, stage, *, dates, batch, width,
):
    _, rows, cols = sre.shape
    odd, _, _ = place()
    stage[...] = jnp.zeros_like(stage)
    boxes = make_boxes(rows, stage, band_ref)
    fields = (sre, sim, hre, him, power)
    load = loader(dates, cols, width, boxes, fields)
    load(mine_ref, 0, edge_mine_ref[...], (3 + odd) * dates)
    load(mate_ref, 0, edge_mate_ref[...], (4 - odd) * dates)
    are[...] = jnp.ones_like(are)
    aim[...] = jnp.zeros_like(aim)
    cohere(boxes, fields, (are, aim), list_i, list_j, cre, cim, 0, counts[0, 0], batch)


def mid_kernel(list_i, list_j, counts, band_ref, cross_ref, za_ref, *refs, batch, width, dates, mid_at):
    sre, sim, hre, him, power, are, aim, cre, cim, stage = refs[9:]
    _, rows, cols = sre.shape
    tiles = 2 * dates + 1
    odd, far, _ = place()
    stage[...] = jnp.zeros_like(stage)
    boxes = make_boxes(rows, stage, band_ref)
    fields = (sre, sim, hre, him, power)
    load = loader(dates, cols, width, boxes, fields)
    up = 5 - 4 * far
    load(cross_ref, 0, cross_ref[tiles - 1], 7 * odd * dates)
    load(za_ref, 0, za_ref[tiles - 1], (up + odd) * dates)
    load(za_ref, tiles, za_ref[2 * tiles - 1], (up + 1 - odd) * dates)
    cohere(boxes, fields, (are, aim), list_i, list_j, cre, cim, mid_at, counts[0, 1], batch)


def link_kernel(
    list_i, list_j, second, third, counts, band_ref, zb_ref, *refs,
    batch, unroll, width, late_at,
):
    out_ref, sre, sim, hre, him, power, are, aim, cre, cim, bre, bim, stage = refs[9:]
    _, dates, rows, cols = out_ref.shape
    tiles = 2 * dates + 1
    odd, far, _ = place()
    own = (3 + odd) * dates
    stage[...] = jnp.zeros_like(stage)
    boxes = make_boxes(rows, stage, band_ref)
    fields = (sre, sim, hre, him, power)
    load = loader(dates, cols, width, boxes, fields)
    others, n2, n3 = counts[0, 2], counts[0, 3], counts[0, 4]
    down = 1 + 4 * far
    load(zb_ref, 0, zb_ref[tiles - 1], (down + odd) * dates)
    load(zb_ref, tiles, zb_ref[2 * tiles - 1], (down + 1 - odd) * dates)
    cohere(boxes, fields, (are, aim), list_i, list_j, cre, cim, late_at, others, batch)

    def scaled(re, im):
        scale = lax.rsqrt(jnp.maximum(re * re + im * im, 1.0))
        return re * scale, im * scale

    def settle(low, count, xr, xi, yr, yi):
        def one(q, carry):
            for u in range(width):
                w = low + width * q + u
                re, im = scaled(xr[w], xi[w])
                xr[w] = re
                xi[w] = im
                yr[w] = re
                yi[w] = im
            return carry

        lax.fori_loop(0, count // width, one, 0)

    def step(index, count, xr, xi, yr, yi):
        def several(first):
            for u in range(unroll):
                p = index[0, first + u]
                i, j = list_i[0, p], list_j[0, p]
                re, im = cre[p], cim[p]
                nr, ni, fr, fi = xr[i], xi[i], xr[j], xi[j]
                ri, rj, ii, ij = yr[i], yr[j], yi[i], yi[j]
                yr[i] = ri + (re * fr - im * fi)
                yr[j] = rj + (re * nr + im * ni)
                yi[i] = ii + (re * fi + im * fr)
                yi[j] = ij + (re * ni - im * nr)

        groups(0, count, unroll, several)

    settle(own - 2 * dates, 5 * dates, are, aim, bre, bim)
    step(second, n2, are, aim, bre, bim)
    settle(own - dates, 3 * dates, bre, bim, are, aim)
    step(third, n3, bre, bim, are, aim)
    for k in range(dates):
        re, im = scaled(are[own + k], aim[own + k])
        out_ref[0, k] = re
        out_ref[1, k] = im


def swap(array, axis, matching):
    matched = {i for pair in matching for i in pair}
    alone = [i for i in range(lax.axis_size(axis)) if i not in matched]
    pairing = [*matching, *zip(alone[::2], alone[1::2], strict=True)]
    return lax.ppermute(array, axis, [*pairing, *((j, i) for i, j in pairing)])


def on_device(slc, pairs):
    comps, dates, rows, cols = slc.shape
    size = lax.axis_size("date")
    pair_count = pairs.shape[0]
    assert lax.axis_size("pix") == 2 and size % 2 == 0 and cols == LANES
    assert GAP <= dates and dates % 2 == 0 and comps * dates * WIN <= cols and rows % 8 == 0

    vmem = pl.BlockSpec(memory_space=pltpu.VMEM)
    smem = pl.BlockSpec(memory_space=pltpu.SMEM)

    def held(array):
        return pltpu.with_memory_space_constraint(array, pltpu.VMEM)

    def matching(step, keep):
        return [(i, i + step) for i in range(size - step) if keep(i)]

    small = pltpu.CompilerParams(vmem_limit_bytes=4 * 1024 * 1024)
    main = slc.reshape(comps * dates, rows, cols)
    mates = matching(1, lambda i: i % 2 == 0)
    mate = swap(main, "date", mates)
    near, edge = pl.pallas_call(
        pack_edges,
        out_shape=[pltpu.VMEM(main.shape, slc.dtype), pltpu.VMEM((rows, cols), slc.dtype)],
        in_specs=[vmem],
        out_specs=[vmem] * 2,
        compiler_params=small,
    )(main)
    edge_mine = swap(edge, "pix", [(0, 1)])
    edge_mate = swap(edge, ("date", "pix"), [(2 * i + p, 2 * j + 1 - p) for i, j in mates for p in (0, 1)])
    cross = jnp.concatenate([near, edge_mine[None]], axis=0)
    both = jnp.concatenate([cross, mate, edge_mate[None]], axis=0)
    cross = swap(cross, "date", matching(3, lambda i: i % 2 == 1))
    za = swap(both, "date", matching(2, lambda i: i // 2 % 2 == 0))
    zb = swap(both, "date", matching(2, lambda i: i // 2 % 2 == 1))

    unroll = max(1, 128 // rows)
    batch = max(1, 128 // rows)
    width = max(w for w in range(1, 2 * unroll + 1) if dates % w == 0)
    per_block = min(pair_count, 2 * pair_count // size)
    mid_at = min(pair_count, 2 * per_block) + SPARE * unroll
    late_at = mid_at + min(pair_count, 4 * per_block) + SPARE * unroll
    cap = late_at + min(pair_count, 4 * per_block) + SPARE * unroll
    window = 8 * dates + 1
    stage = pltpu.VMEM((16 + max(width, 4 * batch) * (rows + 8), cols), jnp.float32)
    plane = 4 * rows * cols
    spare = 4 * 1024 * 1024 + 64 * plane
    length = -(-max(cap, pair_count + unroll) // LANES) * LANES
    lanes = -(-pair_count // LANES) * LANES
    chosen = pl.pallas_call(
        functools.partial(select_kernel, dates=dates, mid_at=mid_at, late_at=late_at, cap=cap),
        out_shape=[pltpu.SMEM((1, length), jnp.int32)] * 5 + [pltpu.VMEM((2 * cols, cols), jnp.bfloat16)],
        in_specs=[vmem],
        out_specs=[smem] * 5 + [vmem],
        scratch_shapes=[pltpu.VMEM((8, lanes), jnp.int32)]
        + [pltpu.VMEM((1, length), jnp.int32)] * 5
        + [pltpu.SemaphoreType.DMA((5,))],
        compiler_params=small,
    )
    lists = chosen(pairs.T)
    band = held(lists[5])
    lists = [pltpu.with_memory_space_constraint(v, pltpu.SMEM) for v in lists[:5]]
    fields = [pltpu.VMEM((window, rows, cols), jnp.float32)] * 7 + [pltpu.VMEM((cap, rows, cols), jnp.float32)] * 2
    local = pl.pallas_call(
        functools.partial(near_kernel, dates=dates, batch=batch, width=width),
        out_shape=fields,
        in_specs=[smem] * 3 + [vmem] * 5,
        out_specs=[vmem] * 9,
        scratch_shapes=[stage],
        compiler_params=pltpu.CompilerParams(vmem_limit_bytes=spare),
    )(lists[0], lists[1], lists[4], band, held(near), held(mate), held(edge_mine), held(edge_mate))
    local = pl.pallas_call(
        functools.partial(mid_kernel, batch=batch, width=width, dates=dates, mid_at=mid_at),
        out_shape=fields,
        in_specs=[smem] * 3 + [vmem] * 12,
        out_specs=[vmem] * 9,
        input_output_aliases={6 + k: k for k in range(9)},
        scratch_shapes=[stage],
        compiler_params=pltpu.CompilerParams(vmem_limit_bytes=spare),
    )(lists[0], lists[1], lists[4], band, held(cross), held(za), *(held(v) for v in local))
    linked = pl.pallas_call(
        functools.partial(link_kernel, batch=batch, unroll=unroll, width=width, late_at=late_at),
        out_shape=[jax.ShapeDtypeStruct((comps, dates, rows, cols), jnp.float32), *fields],
        in_specs=[smem] * 5 + [vmem] * 11,
        out_specs=[vmem] * 10,
        input_output_aliases={7 + k: 1 + k for k in range(9)},
        scratch_shapes=[fields[0]] * 2 + [stage],
        compiler_params=pltpu.CompilerParams(vmem_limit_bytes=spare + 2 * window * plane),
    )(*lists, band, held(zb), *(held(v) for v in local))
    return linked[0]


def solution(mesh):
    in_specs = (P(None, ("grp", "date"), None, "pix"), P("grp", None))
    out_specs = P(None, ("grp", "date"), None, "pix")

    return jax.shard_map(on_device, mesh=mesh, in_specs=in_specs, out_specs=out_specs, check_vma=False)
```

```python
import functools

import jax
import jax.numpy as jnp
from jax import lax
from jax.experimental import pallas as pl
from jax.experimental.pallas import tpu as pltpu
from jax.sharding import PartitionSpec as P


WIN = 2
GAP = 10
LANES = 128
SPARE = 3


def pack_edges(slc_ref, near_ref, edge_ref):
    tiles, rows, cols = slc_ref.shape
    lead = (1 - lax.axis_index("pix")) * WIN
    lane = lax.broadcasted_iota(jnp.int32, (rows, cols), 1)
    acc = jnp.zeros((rows, cols), jnp.float32)
    for t in range(tiles):
        moved = pltpu.roll(slc_ref[t].astype(jnp.float32), lead + WIN * t, 1)
        acc = jnp.where((lane >= WIN * t) & (lane < WIN * (t + 1)), moved, acc)
    near_ref[...] = slc_ref[...]
    edge_ref[...] = acc.astype(edge_ref.dtype)


def place():
    block = lax.axis_index("date")
    return block % 2, (block // 2) % 2, block // 2


def select_kernel(pairs_ref, *refs, dates, mid_at, late_at, cap):
    outs, band_ref, padded, staged, sems = refs[:5], refs[5], refs[6], refs[7:12], refs[12]
    cols = band_ref.shape[1]
    odd, far, chip = place()
    own, inner, last = (3 + odd) * dates, 3 * dates, (1 + 4 * far) * dates
    row = lax.broadcasted_iota(jnp.int32, band_ref.shape, 0)
    column = lax.broadcasted_iota(jnp.int32, band_ref.shape, 1)
    apart = jnp.where(row < cols, row, row - 2 * cols * lax.axis_index("pix")) - column
    band_ref[...] = jnp.where((apart <= WIN) & (apart >= -WIN), 1.0, 0.0).astype(band_ref.dtype)

    lanes, length = padded.shape[1], staged[0].shape[1]
    padded[...] = jnp.full(padded.shape, -(2**20), jnp.int32)
    padded[pl.ds(0, 2), pl.ds(0, pairs_ref.shape[1])] = pairs_ref[...]
    dated = padded[...] - dates * (2 * chip - 3)
    i, j = dated[0:1], dated[1:2]

    def flag(condition):
        return jnp.where(condition, 1.0, 0.0)

    def within(reach):
        return flag(j >= own - reach * dates) * flag(i < own + (reach + 1) * dates)

    def absent(date):
        return 1.0 - flag(date >= last) * flag(date < last + 2 * dates)

    near = flag(i >= inner) * flag(j < inner + 2 * dates)
    wanted = within(2)
    soon = wanted * absent(i) * absent(j)
    classes = [near, soon - near, wanted - soon, within(1), within(0)]
    empty = jnp.zeros((1, lanes), jnp.float32)
    stack = jnp.concatenate([*classes, empty, empty, empty], axis=0)
    before = flag(
        lax.broadcasted_iota(jnp.int32, (lanes, lanes), 0) < lax.broadcasted_iota(jnp.int32, (lanes, lanes), 1)
    ).astype(jnp.bfloat16)
    ranks = jnp.dot(stack.astype(jnp.bfloat16), before, preferred_element_type=jnp.float32)
    rank = [ranks[k : k + 1] for k in range(5)]
    where = classes[0] * rank[0] + classes[1] * (rank[1] + mid_at) + classes[2] * (rank[2] + late_at)
    targets = [where + wanted - 1.0, classes[3] * (rank[3] + 1.0) - 1.0, classes[4] * (rank[4] + 1.0) - 1.0]
    upright = jnp.transpose(jnp.concatenate([*targets, *[empty] * 5], axis=0))
    slots = lax.broadcasted_iota(jnp.int32, (lanes, length), 1).astype(jnp.float32)
    ones = jnp.ones((1, lanes), jnp.float32)
    upper = jnp.floor(where * (1.0 / 128.0))

    def scatter(k, values):
        hot = flag(upright[:, k : k + 1] == slots).astype(jnp.bfloat16)
        rows = jnp.concatenate([*values, *[empty] * (8 - len(values))], axis=0).astype(jnp.bfloat16)
        return jnp.dot(rows, hot, preferred_element_type=jnp.float32)

    ends = scatter(0, [i.astype(jnp.float32) * wanted, j.astype(jnp.float32) * wanted, ones])
    free = 8.0 * dates * (1.0 - ends[2:3])
    staged[0][...] = (ends[0:1] + free).astype(jnp.int32)
    staged[1][...] = (ends[1:2] + free).astype(jnp.int32)
    for k in (1, 2):
        index = scatter(k, [upper, where - 128.0 * upper, ones])
        spot = 128.0 * index[0:1] + index[1:2] + (cap - 1.0) * (1.0 - index[2:3])
        staged[1 + k][...] = spot.astype(jnp.int32)
    sums = jnp.broadcast_to(jnp.sum(stack, axis=1, keepdims=True), (8, length))
    own_lane = flag(
        lax.broadcasted_iota(jnp.int32, (8, length), 0) == lax.broadcasted_iota(jnp.int32, (8, length), 1)
    )
    staged[4][...] = jnp.sum(sums * own_lane, axis=0, keepdims=True).astype(jnp.int32)
    copies = [pltpu.make_async_copy(staged[k], outs[k], sems.at[k]) for k in range(5)]
    for copy in copies:
        copy.start()
    for copy in copies:
        copy.wait()


def make_boxes(rows, stage, band_ref):
    pitch = rows + 8

    def spread(centers, halos, slot):
        values = jnp.concatenate([jnp.concatenate(centers, axis=0), jnp.concatenate(halos, axis=0)], axis=1)
        high = values.astype(jnp.bfloat16)
        low = (values - high.astype(jnp.float32)).astype(jnp.bfloat16)
        band = band_ref[...]
        wide = jnp.dot(high, band, preferred_element_type=jnp.float32)
        wide = wide + jnp.dot(low, band, preferred_element_type=jnp.float32)
        for k in range(len(centers)):
            stage[pl.ds(8 + (slot + k) * pitch, rows), :] = wide[k * rows : (k + 1) * rows]

    def gather(slot):
        start = 8 + slot * pitch
        result = stage[pl.ds(start, rows), :]
        for shift in range(1, WIN + 1):
            result = result + stage[pl.ds(start - shift, rows), :]
            result = result + stage[pl.ds(start + shift, rows), :]
        return result

    return spread, gather


def loader(dates, cols, width, boxes, fields):
    sre, sim, hre, him, power = fields
    spread, gather = boxes
    pix = lax.axis_index("pix")

    def load(ref, first, edge, target):
        edge = pltpu.roll(edge.astype(jnp.float32), -WIN * pix & (cols - 1), 1)
        for start in range(0, dates, width):
            squares, rims = [], []
            for k in range(start, start + width):
                re = ref[first + k].astype(jnp.float32)
                im = ref[first + dates + k].astype(jnp.float32)
                hr = pltpu.roll(edge, -WIN * k & (cols - 1), 1)
                hi = pltpu.roll(edge, -WIN * (dates + k) & (cols - 1), 1)
                sre[target + k] = re
                sim[target + k] = im
                hre[target + k] = hr
                him[target + k] = hi
                squares.append(re * re + im * im)
                rims.append(hr * hr + hi * hi)
            spread(squares, rims, 0)
            for u in range(width):
                power[target + start + u] = gather(u)

    return load


def cohere(boxes, fields, sums, list_i, list_j, cre, cim, first, count, width):
    sre, sim, hre, him, power = fields
    are, aim = sums
    spread, gather = boxes

    def cross(fr, fi, sr, si):
        return [fr * sr + fi * si, fi * sr - fr * si]

    def multiply(group, half):
        centers, halos = [], []
        for u in range(width):
            p = first + group * width + u
            i, j = list_i[0, p], list_j[0, p]
            centers += cross(sre[i], sim[i], sre[j], sim[j])
            halos += cross(hre[i], him[i], hre[j], him[j])
        spread(centers, halos, 2 * width * half)

    def finish(group, half):
        for u in range(width):
            p = first + group * width + u
            i, j = list_i[0, p], list_j[0, p]
            scale = 2.0 / (power[i] + power[j])
            slot = 2 * (width * half + u)
            re, im = gather(slot) * scale, gather(slot + 1) * scale
            cre[p] = re
            cim[p] = im
            ri, rj, ii, ij = are[i], are[j], aim[i], aim[j]
            are[i] = ri + re
            are[j] = rj + re
            aim[i] = ii + im
            aim[j] = ij - im

    def two(q, carry):
        multiply(2 * q + 1, 1)
        finish(2 * q, 0)
        multiply(2 * q + 2, 0)
        finish(2 * q + 1, 1)
        return carry

    multiply(0, 0)
    lax.fori_loop(0, (count + 2 * width - 1) // (2 * width), two, 0)


def groups(first, count, width, body):
    def one(q, carry):
        body(first + q * width)
        return carry

    lax.fori_loop(0, (count + width - 1) // width, one, 0)


def near_kernel(
    list_i, list_j, counts, band_ref, mine_ref, mate_ref, edge_mine_ref, edge_mate_ref,
    sre, sim, hre, him, power, are, aim, cre, cim, stage, *, dates, batch, width,
):
    _, rows, cols = sre.shape
    odd, _, _ = place()
    stage[...] = jnp.zeros_like(stage)
    boxes = make_boxes(rows, stage, band_ref)
    fields = (sre, sim, hre, him, power)
    load = loader(dates, cols, width, boxes, fields)
    load(mine_ref, 0, edge_mine_ref[...], (3 + odd) * dates)
    load(mate_ref, 0, edge_mate_ref[...], (4 - odd) * dates)
    are[...] = jnp.ones_like(are)
    aim[...] = jnp.zeros_like(aim)
    cohere(boxes, fields, (are, aim), list_i, list_j, cre, cim, 0, counts[0, 0], batch)


def mid_kernel(list_i, list_j, counts, band_ref, cross_ref, za_ref, *refs, batch, width, dates, mid_at):
    sre, sim, hre, him, power, are, aim, cre, cim, stage = refs[9:]
    _, rows, cols = sre.shape
    tiles = 2 * dates + 1
    odd, far, _ = place()
    stage[...] = jnp.zeros_like(stage)
    boxes = make_boxes(rows, stage, band_ref)
    fields = (sre, sim, hre, him, power)
    load = loader(dates, cols, width, boxes, fields)
    up = 5 - 4 * far
    load(cross_ref, 0, cross_ref[tiles - 1], 7 * odd * dates)
    load(za_ref, 0, za_ref[tiles - 1], (up + odd) * dates)
    load(za_ref, tiles, za_ref[2 * tiles - 1], (up + 1 - odd) * dates)
    cohere(boxes, fields, (are, aim), list_i, list_j, cre, cim, mid_at, counts[0, 1], batch)


def link_kernel(
    list_i, list_j, second, third, counts, band_ref, zb_ref, *refs,
    batch, unroll, width, late_at,
):
    out_ref, sre, sim, hre, him, power, are, aim, cre, cim, bre, bim, stage = refs[9:]
    _, dates, rows, cols = out_ref.shape
    tiles = 2 * dates + 1
    odd, far, _ = place()
    own = (3 + odd) * dates
    stage[...] = jnp.zeros_like(stage)
    boxes = make_boxes(rows, stage, band_ref)
    fields = (sre, sim, hre, him, power)
    load = loader(dates, cols, width, boxes, fields)
    others, n2, n3 = counts[0, 2], counts[0, 3], counts[0, 4]
    down = 1 + 4 * far

    @pl.when(others > 0)
    def _():
        load(zb_ref, 0, zb_ref[tiles - 1], (down + odd) * dates)
        load(zb_ref, tiles, zb_ref[2 * tiles - 1], (down + 1 - odd) * dates)
        cohere(boxes, fields, (are, aim), list_i, list_j, cre, cim, late_at, others, batch)


    def scaled(re, im):
        scale = lax.rsqrt(jnp.maximum(re * re + im * im, 1.0))
        return re * scale, im * scale

    def settle(low, count, xr, xi, yr, yi):
        def one(q, carry):
            for u in range(width):
                w = low + width * q + u
                re, im = scaled(xr[w], xi[w])
                xr[w] = re
                xi[w] = im
                yr[w] = re
                yi[w] = im
            return carry

        lax.fori_loop(0, count // width, one, 0)

    def step(index, count, xr, xi, yr, yi):
        def several(first):
            for u in range(unroll):
                p = index[0, first + u]
                i, j = list_i[0, p], list_j[0, p]
                re, im = cre[p], cim[p]
                nr, ni, fr, fi = xr[i], xi[i], xr[j], xi[j]
                ri, rj, ii, ij = yr[i], yr[j], yi[i], yi[j]
                yr[i] = ri + (re * fr - im * fi)
                yr[j] = rj + (re * nr + im * ni)
                yi[i] = ii + (re * fi + im * fr)
                yi[j] = ij + (re * ni - im * nr)

        groups(0, count, unroll, several)

    settle(own - 2 * dates, 5 * dates, are, aim, bre, bim)
    step(second, n2, are, aim, bre, bim)
    settle(own - dates, 3 * dates, bre, bim, are, aim)
    step(third, n3, bre, bim, are, aim)
    for k in range(dates):
        re, im = scaled(are[own + k], aim[own + k])
        out_ref[0, k] = re
        out_ref[1, k] = im


def swap(array, axis, matching):
    pairing = matching
    if axis == "date":
        axis, halves = ("date", "pix"), range(2)
        matched = {i for pair in matching for i in pair}
        alone = [i for i in range(lax.axis_size("date")) if i not in matched]
        pairing = [(2 * i + p, 2 * j + p) for i, j in matching for p in halves]
        pairing += [(2 * i, 2 * i + 1) for i in alone]
    return lax.ppermute(array, axis, [*pairing, *((j, i) for i, j in pairing)])


def on_device(slc, pairs):
    comps, dates, rows, cols = slc.shape
    size = lax.axis_size("date")
    pair_count = pairs.shape[0]
    assert lax.axis_size("pix") == 2 and size % 2 == 0 and cols == LANES
    assert GAP <= dates and dates % 2 == 0 and comps * dates * WIN <= cols and rows % 8 == 0

    vmem = pl.BlockSpec(memory_space=pltpu.VMEM)
    smem = pl.BlockSpec(memory_space=pltpu.SMEM)

    def held(array):
        return pltpu.with_memory_space_constraint(array, pltpu.VMEM)

    def matching(step, keep):
        return [(i, i + step) for i in range(size - step) if keep(i)]

    small = pltpu.CompilerParams(vmem_limit_bytes=4 * 1024 * 1024)
    main = slc.reshape(comps * dates, rows, cols)
    mates = matching(1, lambda i: i % 2 == 0)
    mate = swap(main, "date", mates)
    near, edge = pl.pallas_call(
        pack_edges,
        out_shape=[pltpu.VMEM(main.shape, slc.dtype), pltpu.VMEM((rows, cols), slc.dtype)],
        in_specs=[vmem],
        out_specs=[vmem] * 2,
        compiler_params=small,
    )(main)
    edge_mine = swap(edge, "pix", [(0, 1)])
    edge_mate = swap(edge, ("date", "pix"), [(2 * i + p, 2 * j + 1 - p) for i, j in mates for p in (0, 1)])
    cross = jnp.concatenate([near, edge_mine[None]], axis=0)
    both = jnp.concatenate([cross, mate, edge_mate[None]], axis=0)
    cross = swap(cross, "date", matching(3, lambda i: i % 2 == 1))
    za = swap(both, "date", matching(2, lambda i: i // 2 % 2 == 0))
    zb = swap(both, "date", matching(2, lambda i: i // 2 % 2 == 1))

    unroll = max(1, 128 // rows)
    batch = max(1, 128 // rows)
    width = max(w for w in range(1, 2 * unroll + 1) if dates % w == 0)
    per_block = min(pair_count, 2 * pair_count // size)
    mid_at = min(pair_count, 2 * per_block) + SPARE * unroll
    late_at = mid_at + min(pair_count, 4 * per_block) + SPARE * unroll
    cap = late_at + min(pair_count, 4 * per_block) + SPARE * unroll
    window = 8 * dates + 1
    stage = pltpu.VMEM((16 + max(width, 4 * batch) * (rows + 8), cols), jnp.float32)
    plane = 4 * rows * cols
    spare = 4 * 1024 * 1024 + 64 * plane
    length = -(-max(cap, pair_count + unroll) // LANES) * LANES
    lanes = -(-pair_count // LANES) * LANES
    chosen = pl.pallas_call(
        functools.partial(select_kernel, dates=dates, mid_at=mid_at, late_at=late_at, cap=cap),
        out_shape=[pltpu.SMEM((1, length), jnp.int32)] * 5 + [pltpu.VMEM((2 * cols, cols), jnp.bfloat16)],
        in_specs=[vmem],
        out_specs=[smem] * 5 + [vmem],
        scratch_shapes=[pltpu.VMEM((8, lanes), jnp.int32)]
        + [pltpu.VMEM((1, length), jnp.int32)] * 5
        + [pltpu.SemaphoreType.DMA((5,))],
        compiler_params=small,
    )
    lists = chosen(pairs.T)
    band = held(lists[5])
    lists = [pltpu.with_memory_space_constraint(v, pltpu.SMEM) for v in lists[:5]]
    fields = [pltpu.VMEM((window, rows, cols), jnp.float32)] * 7 + [pltpu.VMEM((cap, rows, cols), jnp.float32)] * 2
    local = pl.pallas_call(
        functools.partial(near_kernel, dates=dates, batch=batch, width=width),
        out_shape=fields,
        in_specs=[smem] * 3 + [vmem] * 5,
        out_specs=[vmem] * 9,
        scratch_shapes=[stage],
        compiler_params=pltpu.CompilerParams(vmem_limit_bytes=spare),
    )(lists[0], lists[1], lists[4], band, held(near), held(mate), held(edge_mine), held(edge_mate))
    local = pl.pallas_call(
        functools.partial(mid_kernel, batch=batch, width=width, dates=dates, mid_at=mid_at),
        out_shape=fields,
        in_specs=[smem] * 3 + [vmem] * 12,
        out_specs=[vmem] * 9,
        input_output_aliases={6 + k: k for k in range(9)},
        scratch_shapes=[stage],
        compiler_params=pltpu.CompilerParams(vmem_limit_bytes=spare),
    )(lists[0], lists[1], lists[4], band, held(cross), held(za), *(held(v) for v in local))
    linked = pl.pallas_call(
        functools.partial(link_kernel, batch=batch, unroll=unroll, width=width, late_at=late_at),
        out_shape=[jax.ShapeDtypeStruct((comps, dates, rows, cols), jnp.float32), *fields],
        in_specs=[smem] * 5 + [vmem] * 11,
        out_specs=[vmem] * 10,
        input_output_aliases={7 + k: 1 + k for k in range(9)},
        scratch_shapes=[fields[0]] * 2 + [stage],
        compiler_params=pltpu.CompilerParams(vmem_limit_bytes=spare + 2 * window * plane),
    )(*lists, band, held(zb), *(held(v) for v in local))
    return linked[0]


def solution(mesh):
    in_specs = (P(None, ("grp", "date"), None, "pix"), P("grp", None))
    out_specs = P(None, ("grp", "date"), None, "pix")

    return jax.shard_map(on_device, mesh=mesh, in_specs=in_specs, out_specs=out_specs, check_vma=False)
```

```python
import functools

import jax
import jax.numpy as jnp
from jax import lax
from jax.experimental import pallas as pl
from jax.experimental.pallas import tpu as pltpu
from jax.sharding import PartitionSpec as P


WIN = 2
GAP = 10
LANES = 128
SPARE = 3


def pack_edges(slc_ref, near_ref, edge_ref):
    tiles, rows, cols = slc_ref.shape
    lead = (1 - lax.axis_index("pix")) * WIN
    lane = lax.broadcasted_iota(jnp.int32, (rows, cols), 1)
    acc = jnp.zeros((rows, cols), jnp.float32)
    for t in range(tiles):
        moved = pltpu.roll(slc_ref[t].astype(jnp.float32), lead + WIN * t, 1)
        acc = jnp.where((lane >= WIN * t) & (lane < WIN * (t + 1)), moved, acc)
    near_ref[...] = slc_ref[...]
    edge_ref[...] = acc.astype(edge_ref.dtype)


def place():
    block = lax.axis_index("date")
    return block % 2, (block // 2) % 2, block // 2


def select_kernel(pairs_ref, *refs, dates, mid_at, late_at, cap):
    outs, band_ref, padded, staged, sems = refs[:5], refs[5], refs[6], refs[7:12], refs[12]
    cols = band_ref.shape[1]
    odd, far, chip = place()
    own, inner, last = (3 + odd) * dates, 3 * dates, (1 + 4 * far) * dates
    row = lax.broadcasted_iota(jnp.int32, band_ref.shape, 0)
    column = lax.broadcasted_iota(jnp.int32, band_ref.shape, 1)
    apart = jnp.where(row < cols, row, row - 2 * cols * lax.axis_index("pix")) - column
    band_ref[...] = jnp.where((apart <= WIN) & (apart >= -WIN), 1.0, 0.0).astype(band_ref.dtype)

    lanes, length = padded.shape[1], staged[0].shape[1]
    padded[...] = jnp.full(padded.shape, -(2**20), jnp.int32)
    padded[pl.ds(0, 2), pl.ds(0, pairs_ref.shape[1])] = pairs_ref[...]
    dated = padded[...] - dates * (2 * chip - 3)
    i, j = dated[0:1], dated[1:2]

    def flag(condition):
        return jnp.where(condition, 1.0, 0.0)

    def within(reach):
        return flag(j >= own - reach * dates) * flag(i < own + (reach + 1) * dates)

    def absent(date):
        return 1.0 - flag(date >= last) * flag(date < last + 2 * dates)

    near = flag(i >= inner) * flag(j < inner + 2 * dates)
    wanted = within(2)
    soon = wanted * absent(i) * absent(j)
    classes = [near, soon - near, wanted - soon, within(1), within(0)]
    empty = jnp.zeros((1, lanes), jnp.float32)
    stack = jnp.concatenate([*classes, empty, empty, empty], axis=0)
    before = flag(
        lax.broadcasted_iota(jnp.int32, (lanes, lanes), 0) < lax.broadcasted_iota(jnp.int32, (lanes, lanes), 1)
    ).astype(jnp.bfloat16)
    ranks = jnp.dot(stack.astype(jnp.bfloat16), before, preferred_element_type=jnp.float32)
    rank = [ranks[k : k + 1] for k in range(5)]
    where = classes[0] * rank[0] + classes[1] * (rank[1] + mid_at) + classes[2] * (rank[2] + late_at)
    targets = [where + wanted - 1.0, classes[3] * (rank[3] + 1.0) - 1.0, classes[4] * (rank[4] + 1.0) - 1.0]
    upright = jnp.transpose(jnp.concatenate([*targets, *[empty] * 5], axis=0))
    slots = lax.broadcasted_iota(jnp.int32, (lanes, length), 1).astype(jnp.float32)
    ones = jnp.ones((1, lanes), jnp.float32)
    upper = jnp.floor(where * (1.0 / 128.0))

    def scatter(k, values):
        hot = flag(upright[:, k : k + 1] == slots).astype(jnp.bfloat16)
        rows = jnp.concatenate([*values, *[empty] * (8 - len(values))], axis=0).astype(jnp.bfloat16)
        return jnp.dot(rows, hot, preferred_element_type=jnp.float32)

    ends = scatter(0, [i.astype(jnp.float32) * wanted, j.astype(jnp.float32) * wanted, ones])
    free = 8.0 * dates * (1.0 - ends[2:3])
    staged[0][...] = (ends[0:1] + free).astype(jnp.int32)
    staged[1][...] = (ends[1:2] + free).astype(jnp.int32)
    for k in (1, 2):
        index = scatter(k, [upper, where - 128.0 * upper, ones])
        spot = 128.0 * index[0:1] + index[1:2] + (cap - 1.0) * (1.0 - index[2:3])
        staged[1 + k][...] = spot.astype(jnp.int32)
    sums = jnp.broadcast_to(jnp.sum(stack, axis=1, keepdims=True), (8, length))
    own_lane = flag(
        lax.broadcasted_iota(jnp.int32, (8, length), 0) == lax.broadcasted_iota(jnp.int32, (8, length), 1)
    )
    staged[4][...] = jnp.sum(sums * own_lane, axis=0, keepdims=True).astype(jnp.int32)
    copies = [pltpu.make_async_copy(staged[k], outs[k], sems.at[k]) for k in range(5)]
    for copy in copies:
        copy.start()
    for copy in copies:
        copy.wait()


def make_boxes(rows, stage, band_ref):
    pitch = rows + 8

    def spread(centers, halos, slot):
        values = jnp.concatenate([jnp.concatenate(centers, axis=0), jnp.concatenate(halos, axis=0)], axis=1)
        high = values.astype(jnp.bfloat16)
        low = (values - high.astype(jnp.float32)).astype(jnp.bfloat16)
        band = band_ref[...]
        wide = jnp.dot(high, band, preferred_element_type=jnp.float32)
        wide = wide + jnp.dot(low, band, preferred_element_type=jnp.float32)
        for k in range(len(centers)):
            stage[pl.ds(8 + (slot + k) * pitch, rows), :] = wide[k * rows : (k + 1) * rows]

    def gather(slot):
        start = 8 + slot * pitch
        result = stage[pl.ds(start, rows), :]
        for shift in range(1, WIN + 1):
            result = result + stage[pl.ds(start - shift, rows), :]
            result = result + stage[pl.ds(start + shift, rows), :]
        return result

    return spread, gather


def loader(dates, cols, width, boxes, fields):
    sre, sim, hre, him, power = fields
    spread, gather = boxes
    pix = lax.axis_index("pix")

    def load(ref, first, edge, target):
        edge = pltpu.roll(edge.astype(jnp.float32), -WIN * pix & (cols - 1), 1)
        for start in range(0, dates, width):
            squares, rims = [], []
            for k in range(start, start + width):
                re = ref[first + k].astype(jnp.float32)
                im = ref[first + dates + k].astype(jnp.float32)
                hr = pltpu.roll(edge, -WIN * k & (cols - 1), 1)
                hi = pltpu.roll(edge, -WIN * (dates + k) & (cols - 1), 1)
                sre[target + k] = re
                sim[target + k] = im
                hre[target + k] = hr
                him[target + k] = hi
                squares.append(re * re + im * im)
                rims.append(hr * hr + hi * hi)
            spread(squares, rims, 0)
            for u in range(width):
                power[target + start + u] = gather(u)

    return load


def cohere(boxes, fields, sums, list_i, list_j, cre, cim, first, count, width):
    sre, sim, hre, him, power = fields
    are, aim = sums
    spread, gather = boxes

    def cross(fr, fi, sr, si):
        return [fr * sr + fi * si, fi * sr - fr * si]

    def multiply(group, half):
        centers, halos = [], []
        for u in range(width):
            p = first + group * width + u
            i, j = list_i[0, p], list_j[0, p]
            centers += cross(sre[i], sim[i], sre[j], sim[j])
            halos += cross(hre[i], him[i], hre[j], him[j])
        spread(centers, halos, 2 * width * half)

    def finish(group, half):
        for u in range(width):
            p = first + group * width + u
            i, j = list_i[0, p], list_j[0, p]
            scale = 2.0 / (power[i] + power[j])
            slot = 2 * (width * half + u)
            re, im = gather(slot) * scale, gather(slot + 1) * scale
            cre[p] = re
            cim[p] = im
            ri, rj, ii, ij = are[i], are[j], aim[i], aim[j]
            are[i] = ri + re
            are[j] = rj + re
            aim[i] = ii + im
            aim[j] = ij - im

    def two(q, carry):
        multiply(2 * q + 1, 1)
        finish(2 * q, 0)
        multiply(2 * q + 2, 0)
        finish(2 * q + 1, 1)
        return carry

    multiply(0, 0)
    lax.fori_loop(0, (count + 2 * width - 1) // (2 * width), two, 0)


def groups(first, count, width, body):
    def one(q, carry):
        body(first + q * width)
        return carry

    lax.fori_loop(0, (count + width - 1) // width, one, 0)


def near_kernel(
    list_i, list_j, counts, band_ref, mine_ref, mate_ref, edge_mine_ref, edge_mate_ref,
    sre, sim, hre, him, power, are, aim, cre, cim, stage, *, dates, batch, width,
):
    _, rows, cols = sre.shape
    odd, _, _ = place()
    stage[...] = jnp.zeros_like(stage)
    boxes = make_boxes(rows, stage, band_ref)
    fields = (sre, sim, hre, him, power)
    load = loader(dates, cols, width, boxes, fields)
    load(mine_ref, 0, edge_mine_ref[...], (3 + odd) * dates)
    load(mate_ref, 0, edge_mate_ref[...], (4 - odd) * dates)
    are[...] = jnp.ones_like(are)
    aim[...] = jnp.zeros_like(aim)
    cohere(boxes, fields, (are, aim), list_i, list_j, cre, cim, 0, counts[0, 0], batch)


def mid_kernel(list_i, list_j, counts, band_ref, cross_ref, za_ref, *refs, batch, width, dates, mid_at):
    sre, sim, hre, him, power, are, aim, cre, cim, stage = refs[9:]
    _, rows, cols = sre.shape
    tiles = 2 * dates + 1
    odd, far, _ = place()
    stage[...] = jnp.zeros_like(stage)
    boxes = make_boxes(rows, stage, band_ref)
    fields = (sre, sim, hre, him, power)
    load = loader(dates, cols, width, boxes, fields)
    up = 5 - 4 * far
    load(cross_ref, 0, cross_ref[tiles - 1], 7 * odd * dates)
    load(za_ref, 0, za_ref[tiles - 1], (up + odd) * dates)
    load(za_ref, tiles, za_ref[2 * tiles - 1], (up + 1 - odd) * dates)
    cohere(boxes, fields, (are, aim), list_i, list_j, cre, cim, mid_at, counts[0, 1], batch)


def link_kernel(
    list_i, list_j, second, third, counts, band_ref, zb_ref, *refs,
    batch, unroll, width, late_at,
):
    out_ref, sre, sim, hre, him, power, are, aim, cre, cim, bre, bim, stage = refs[9:]
    _, dates, rows, cols = out_ref.shape
    tiles = 2 * dates + 1
    odd, far, _ = place()
    own = (3 + odd) * dates
    stage[...] = jnp.zeros_like(stage)
    boxes = make_boxes(rows, stage, band_ref)
    fields = (sre, sim, hre, him, power)
    load = loader(dates, cols, width, boxes, fields)
    others, n2, n3 = counts[0, 2], counts[0, 3], counts[0, 4]
    down = 1 + 4 * far

    @pl.when(others > 0)
    def _():
        load(zb_ref, 0, zb_ref[tiles - 1], (down + odd) * dates)
        load(zb_ref, tiles, zb_ref[2 * tiles - 1], (down + 1 - odd) * dates)

    cohere(boxes, fields, (are, aim), list_i, list_j, cre, cim, late_at, others, batch)

    def scaled(re, im):
        scale = lax.rsqrt(jnp.maximum(re * re + im * im, 1.0))
        return re * scale, im * scale

    def settle(low, count, xr, xi, yr, yi):
        def one(q, carry):
            for u in range(dates):
                w = low + dates * q + u
                re, im = scaled(xr[w], xi[w])
                xr[w] = re
                xi[w] = im
                yr[w] = re
                yi[w] = im
            return carry

        lax.fori_loop(0, count // dates, one, 0)

    def step(index, count, xr, xi, yr, yi):
        def several(first):
            for u in range(unroll):
                p = index[0, first + u]
                i, j = list_i[0, p], list_j[0, p]
                re, im = cre[p], cim[p]
                nr, ni, fr, fi = xr[i], xi[i], xr[j], xi[j]
                ri, rj, ii, ij = yr[i], yr[j], yi[i], yi[j]
                yr[i] = ri + (re * fr - im * fi)
                yr[j] = rj + (re * nr + im * ni)
                yi[i] = ii + (re * fi + im * fr)
                yi[j] = ij + (re * ni - im * nr)

        groups(0, count, unroll, several)

    settle(own - 2 * dates, 5 * dates, are, aim, bre, bim)
    step(second, n2, are, aim, bre, bim)
    settle(own - dates, 3 * dates, bre, bim, are, aim)
    step(third, n3, bre, bim, are, aim)
    for k in range(dates):
        re, im = scaled(are[own + k], aim[own + k])
        out_ref[0, k] = re
        out_ref[1, k] = im


def swap(array, axis, matching):
    pairing = matching
    if axis == "date":
        axis, halves = ("date", "pix"), range(2)
        matched = {i for pair in matching for i in pair}
        alone = [i for i in range(lax.axis_size("date")) if i not in matched]
        pairing = [(2 * i + p, 2 * j + p) for i, j in matching for p in halves]
        pairing += [(2 * i, 2 * i + 1) for i in alone]
    return lax.ppermute(array, axis, [*pairing, *((j, i) for i, j in pairing)])


def on_device(slc, pairs):
    comps, dates, rows, cols = slc.shape
    size = lax.axis_size("date")
    pair_count = pairs.shape[0]
    assert lax.axis_size("pix") == 2 and size % 2 == 0 and cols == LANES
    assert GAP <= dates and dates % 2 == 0 and comps * dates * WIN <= cols and rows % 8 == 0

    vmem = pl.BlockSpec(memory_space=pltpu.VMEM)
    smem = pl.BlockSpec(memory_space=pltpu.SMEM)

    def held(array):
        return pltpu.with_memory_space_constraint(array, pltpu.VMEM)

    def matching(step, keep):
        return [(i, i + step) for i in range(size - step) if keep(i)]

    small = pltpu.CompilerParams(vmem_limit_bytes=4 * 1024 * 1024)
    main = slc.reshape(comps * dates, rows, cols)
    mates = matching(1, lambda i: i % 2 == 0)
    mate = swap(main, "date", mates)
    near, edge = pl.pallas_call(
        pack_edges,
        out_shape=[pltpu.VMEM(main.shape, slc.dtype), pltpu.VMEM((rows, cols), slc.dtype)],
        in_specs=[vmem],
        out_specs=[vmem] * 2,
        compiler_params=small,
    )(main)
    edge_mine = swap(edge, "pix", [(0, 1)])
    edge_mate = swap(edge, ("date", "pix"), [(2 * i + p, 2 * j + 1 - p) for i, j in mates for p in (0, 1)])
    cross = jnp.concatenate([near, edge_mine[None]], axis=0)
    both = jnp.concatenate([cross, mate, edge_mate[None]], axis=0)
    cross = swap(cross, "date", matching(3, lambda i: i % 2 == 1))
    za = swap(both, "date", matching(2, lambda i: i // 2 % 2 == 0))
    zb = swap(both, "date", matching(2, lambda i: i // 2 % 2 == 1))

    unroll = max(1, 256 // rows)
    batch = max(1, 128 // rows)
    width = max(w for w in range(1, 2 * unroll + 1) if dates % w == 0)
    per_block = min(pair_count, 2 * pair_count // size)
    mid_at = min(pair_count, 2 * per_block) + SPARE * unroll
    late_at = mid_at + min(pair_count, 4 * per_block) + SPARE * unroll
    cap = late_at + min(pair_count, 4 * per_block) + SPARE * unroll
    window = 8 * dates + 1
    stage = pltpu.VMEM((16 + max(width, 4 * batch) * (rows + 8), cols), jnp.float32)
    plane = 4 * rows * cols
    spare = 4 * 1024 * 1024 + 64 * plane
    length = -(-max(cap, pair_count + unroll) // LANES) * LANES
    lanes = -(-pair_count // LANES) * LANES
    chosen = pl.pallas_call(
        functools.partial(select_kernel, dates=dates, mid_at=mid_at, late_at=late_at, cap=cap),
        out_shape=[pltpu.SMEM((1, length), jnp.int32)] * 5 + [pltpu.VMEM((2 * cols, cols), jnp.bfloat16)],
        in_specs=[vmem],
        out_specs=[smem] * 5 + [vmem],
        scratch_shapes=[pltpu.VMEM((8, lanes), jnp.int32)]
        + [pltpu.VMEM((1, length), jnp.int32)] * 5
        + [pltpu.SemaphoreType.DMA((5,))],
        compiler_params=small,
    )
    lists = chosen(pairs.T)
    band = held(lists[5])
    lists = [pltpu.with_memory_space_constraint(v, pltpu.SMEM) for v in lists[:5]]
    fields = [pltpu.VMEM((window, rows, cols), jnp.float32)] * 7 + [pltpu.VMEM((cap, rows, cols), jnp.float32)] * 2
    local = pl.pallas_call(
        functools.partial(near_kernel, dates=dates, batch=batch, width=width),
        out_shape=fields,
        in_specs=[smem] * 3 + [vmem] * 5,
        out_specs=[vmem] * 9,
        scratch_shapes=[stage],
        compiler_params=pltpu.CompilerParams(vmem_limit_bytes=spare),
    )(lists[0], lists[1], lists[4], band, held(near), held(mate), held(edge_mine), held(edge_mate))
    local = pl.pallas_call(
        functools.partial(mid_kernel, batch=batch, width=width, dates=dates, mid_at=mid_at),
        out_shape=fields,
        in_specs=[smem] * 3 + [vmem] * 12,
        out_specs=[vmem] * 9,
        input_output_aliases={6 + k: k for k in range(9)},
        scratch_shapes=[stage],
        compiler_params=pltpu.CompilerParams(vmem_limit_bytes=spare),
    )(lists[0], lists[1], lists[4], band, held(cross), held(za), *(held(v) for v in local))
    linked = pl.pallas_call(
        functools.partial(link_kernel, batch=batch, unroll=unroll, width=width, late_at=late_at),
        out_shape=[jax.ShapeDtypeStruct((comps, dates, rows, cols), jnp.float32), *fields],
        in_specs=[smem] * 5 + [vmem] * 11,
        out_specs=[vmem] * 10,
        input_output_aliases={7 + k: 1 + k for k in range(9)},
        scratch_shapes=[fields[0]] * 2 + [stage],
        compiler_params=pltpu.CompilerParams(vmem_limit_bytes=spare + 2 * window * plane),
    )(*lists, band, held(zb), *(held(v) for v in local))
    return linked[0]


def solution(mesh):
    in_specs = (P(None, ("grp", "date"), None, "pix"), P("grp", None))
    out_specs = P(None, ("grp", "date"), None, "pix")

    return jax.shard_map(on_device, mesh=mesh, in_specs=in_specs, out_specs=out_specs, check_vma=False)
```
